512 devices in a mesh: spec: 16 (over y, x), tile: 32 (over z, core).
Axes of the slice: x: 4, y: 4, z: 16, core: 2. Of those that a mesh axis runs over, the one named last changes fastest.
Arguments:
- action: bfloat16 [512, 3072, 256], P('tile', 'spec'), may hold values from 0.099609375 to 2
- east_current: float32 [512, 256], P('tile'), may hold values from -0.4 to 0.4
- north_current: float32 [512, 256], P('tile'), may hold values from -0.4 to 0.4
- sea_mask: int32 [512, 256], P('tile'), may hold values from 0 to 1, as said below
- pattern: int32 [48, 24], replicated, may hold values from 0 to 47, as said below
- table: bfloat16 [48, 64, 64], replicated, may hold values from -0.15625 to 0.15625
Outputs:
- updated: bfloat16 [512, 3072, 256], P('tile', 'spec')
The draws below stay inside these ranges and needn't reach their ends.
Inputs may be any that keep to these rules, and one draw needn't show every extreme that they name: `sea_mask`: each tile of 16 latitude rows (all 256 longitudes) holds at most 2048 sea points, and in every draw some tile holds exactly 2048. `pattern`: each row names 24 different direction blocks.
All inputs are finite; a program needn't handle non-finite values.
Results may differ from the reference program's by a relative error of at most 0.0043.
Values may be sent and summed in bfloat16 or wider, within the bound.
A program may use at most 64 MiB of HBM per device.

```python
import math
import jax
import jax.numpy as jnp
from jax import lax

NF = 64
ND = 48
K = 3072
R = 24
SUB = 2
ROWS = 16
LON = 256
LAT = 512
SEA_TILE = 2048


def draw_sea_mask(key, part):
    tile_count = LAT // ROWS
    tile_cells = ROWS * LON
    first_key, second_key, third_key = jax.random.split(key, 3)
    counts = jax.random.randint(first_key, (tile_count,), SEA_TILE // 2, SEA_TILE + 1)
    fullest = jax.random.randint(second_key, (), 0, tile_count)
    counts = jnp.where(jnp.arange(tile_count) == fullest, SEA_TILE, counts)
    tile_keys = jax.random.split(third_key, tile_count)
    ranks = jax.vmap(lambda tile_key: jax.random.permutation(tile_key, tile_cells))(tile_keys)
    sea_cells = (ranks < counts[:, None]).astype(jnp.int32)
    return sea_cells.reshape(LAT, LON)


def draw_pattern(key, part):
    row_keys = jax.random.split(jax.random.fold_in(key, 7), ND)
    chosen = jax.vmap(lambda row_key: jax.random.permutation(row_key, ND)[:R])(row_keys)
    return chosen.astype(jnp.int32)


def level_of(stream_key, dims, shards, low, high):
    loudness = 1.0
    for axis_at, blocks in shards:
        draws = jax.random.uniform(jax.random.fold_in(jax.random.fold_in(stream_key, 6), axis_at), (blocks,), jnp.float32, low / len(shards), high / len(shards))
        loudness = loudness * jnp.repeat(jnp.exp(draws), dims[axis_at] // blocks).reshape((-1,) + (1,) * (len(dims) - 1 - axis_at))
    return loudness


def gaussian(key, dims, deviation, reach, kind=jnp.bfloat16):
    drawn = deviation * jax.random.normal(key, dims, jnp.float32)
    return jnp.clip(drawn, min=-reach, max=reach).astype(kind)


def setup_inputs(seed: int = 0) -> dict:
    splits = jax.random.split(jax.random.key(seed), 7)
    action = jnp.clip(jnp.exp(math.log(2.0) - 2.9996462 * jax.random.uniform(splits[0], (LAT, K, LON), jnp.float32) ** level_of(splits[0], (LAT, K, LON), ((0, 32), (1, 16)), -0.2, 0.2)), 0.099609375, 2.0).astype(jnp.bfloat16)
    east_current = jnp.clip(jax.random.uniform(splits[1], (LAT, LON), jnp.float32, -0.4, 0.4) * level_of(splits[1], (LAT, LON), ((0, 32),), -0.4, 0.0), -0.4, 0.4)
    north_current = jnp.clip(jax.random.uniform(splits[2], (LAT, LON), jnp.float32, -0.4, 0.4) * level_of(splits[2], (LAT, LON), ((0, 32),), -0.4, 0.0), -0.4, 0.4)
    sea_mask = draw_sea_mask(jax.random.fold_in(splits[6], 71), 0)
    pattern = draw_pattern(jax.random.fold_in(splits[6], 71), 0)
    table = gaussian(splits[5], (ND, NF, NF), (R * NF) ** -0.5, 0.15625)
    return {"action": action, "east_current": east_current, "north_current": north_current, "sea_mask": sea_mask, "pattern": pattern, "table": table}


courant_scale = 0.45


def upwind(padded, courant_east, courant_north):
    center = padded[1:-1]
    south_row = padded[:-2]
    north_row = padded[2:]
    zero_column = jnp.zeros_like(center[:, :, :1])
    west_cell = jnp.concatenate([zero_column, center[:, :, :-1]], axis=2)
    east_cell = jnp.concatenate([center[:, :, 1:], zero_column], axis=2)
    return (center
            - jnp.maximum(courant_east, 0.0) * (center - west_cell)
            - jnp.minimum(courant_east, 0.0) * (east_cell - center)
            - jnp.maximum(courant_north, 0.0) * (center - south_row)
            - jnp.minimum(courant_north, 0.0) * (north_row - center))


def reference(action, east_current, north_current, sea_mask, pattern, table):
    speed = jnp.exp(-2.0 * jnp.arange(NF, dtype=jnp.float32) / (NF - 1))

    def propagate(direction):
        block = lax.dynamic_slice_in_dim(action, direction * NF, NF, 1).astype(jnp.float32)
        theta = 2.0 * jnp.pi * direction.astype(jnp.float32) / ND
        courant_east = courant_scale * (speed[None, :, None] * jnp.cos(theta) + east_current[:, None, :])
        courant_north = courant_scale * (speed[None, :, None] * jnp.sin(theta) + north_current[:, None, :])
        for substep in range(SUB):
            padded = jnp.pad(block, ((1, 1), (0, 0), (0, 0)))
            block = upwind(padded, courant_east, courant_north)
        return jnp.transpose(block.astype(jnp.bfloat16), (1, 0, 2))

    moved = lax.map(propagate, jnp.arange(ND, dtype=jnp.int32))
    cell_count = LAT * LON
    flat = moved.reshape(ND, NF, cell_count)
    offsets = (pattern - jnp.arange(ND, dtype=jnp.int32)[:, None]) % ND
    weights = table[offsets].astype(jnp.float32)
    mask_flat = sea_mask.reshape(cell_count)
    block_cells = math.gcd(cell_count, 512)

    def source(start):
        piece = lax.dynamic_slice_in_dim(flat, start, block_cells, 2)
        gathered = piece[pattern].astype(jnp.float32)
        coupled = jnp.einsum('rjab,rjbc->rac', weights, gathered)
        own_action = piece.astype(jnp.float32)
        sea_part = lax.dynamic_slice_in_dim(mask_flat, start, block_cells, 0).astype(jnp.float32)
        return (own_action + sea_part[None, None, :] * own_action * coupled).astype(jnp.bfloat16)

    starts = jnp.arange(cell_count // block_cells, dtype=jnp.int32) * block_cells
    blocks_out = lax.map(source, starts)
    result = jnp.moveaxis(blocks_out, 0, 2).reshape(ND * NF, LAT, LON)
    return jnp.transpose(result, (1, 0, 2))
```

```python
import functools
import math

import jax
import jax.numpy as jnp
from jax import lax
from jax.experimental import pallas as pl
from jax.experimental.pallas import tpu as pltpu
from jax.sharding import PartitionSpec as P

NF = 64
ND = 48
GROUPS = 3
SPEC = 16
TILES = 32
ROWS = 16
LON = 256
HALF = 128
WINDOWS = 8
STRIP = 16
COURANT = 0.45
MESH = pl.DeviceIdType.MESH
BF = jnp.bfloat16
F32 = jnp.float32


def iota(shape, dim):
    return lax.broadcasted_iota(jnp.int32, shape, dim)


def dot(a, b, ca=1, cb=0):
    return lax.dot_general(a, b, (((ca,), (cb,)), ((), ())), preferred_element_type=F32)


def step_kernel(
    action, east, north, mask, pattern, table, out,
    halo, current, coef_e, coef_n, moved, slot_row, window_row, mask_row, onehot, windows, ring,
    send, recv, total, weight, pairs, hits, back_send, back_recv,
    halo_send, halo_recv, cur_send, cur_recv, out_send, out_recv, ret_send, ret_recv,
):
    me = lax.axis_index("spec")
    tile = lax.axis_index("tile")
    up = lax.rem(tile + 1, TILES)
    down = lax.rem(tile + TILES - 1, TILES)

    barrier = pltpu.get_barrier_semaphore()

    def greet(i, carry):
        pl.semaphore_signal(
            barrier, inc=1, device_id={"spec": lax.rem(me + i, SPEC)}, device_id_type=MESH
        )
        return carry

    lax.fori_loop(1, SPEC, greet, 0)
    pl.semaphore_signal(barrier, inc=1, device_id={"tile": up}, device_id_type=MESH)
    pl.semaphore_signal(barrier, inc=1, device_id={"tile": down}, device_id_type=MESH)

    for row in range(ROWS):
        current[row + 1, 0] = jnp.broadcast_to(COURANT * east[row : row + 1, :], (8, LON))
        current[row + 1, 1] = jnp.broadcast_to(COURANT * north[row : row + 1, :], (8, LON))

    pl.semaphore_wait(barrier, SPEC + 1)

    cur_up = pltpu.make_async_remote_copy(
        src_ref=current.at[ROWS], dst_ref=current.at[0],
        send_sem=cur_send.at[0], recv_sem=cur_recv.at[0],
        device_id={"tile": up}, device_id_type=MESH,
    )
    cur_down = pltpu.make_async_remote_copy(
        src_ref=current.at[1], dst_ref=current.at[ROWS + 1],
        send_sem=cur_send.at[1], recv_sem=cur_recv.at[1],
        device_id={"tile": down}, device_id_type=MESH,
    )
    cur_up.start()
    cur_down.start()

    def halo_copies(g):
        comps = pl.ds(pl.multiple_of(g * NF, NF), NF)
        to_up = pltpu.make_async_remote_copy(
            src_ref=action.at[pl.ds(ROWS - 2, 2), comps], dst_ref=halo.at[0, :, comps],
            send_sem=halo_send.at[0, g], recv_sem=halo_recv.at[0, g],
            device_id={"tile": up}, device_id_type=MESH,
        )
        to_down = pltpu.make_async_remote_copy(
            src_ref=action.at[pl.ds(0, 2), comps], dst_ref=halo.at[1, :, comps],
            send_sem=halo_send.at[1, g], recv_sem=halo_recv.at[1, g],
            device_id={"tile": down}, device_id_type=MESH,
        )
        return to_up, to_down

    def start_halo(g, carry):
        to_up, to_down = halo_copies(g)
        to_up.start()
        to_down.start()
        return carry

    lax.fori_loop(0, GROUPS, start_halo, 0)

    speed = jnp.exp(iota((NF, HALF), 0).astype(F32) * (-2.0 / (NF - 1)))
    for g in range(GROUPS):
        direction = jnp.full((8, HALF), me * GROUPS + g, jnp.int32).astype(F32)
        theta = direction * (2.0 * math.pi / ND)
        cosine = COURANT * jnp.cos(theta)
        sine = COURANT * jnp.sin(theta)
        for k in range(0, NF, 8):
            coef_e[g * NF + k : g * NF + k + 8, :] = speed[k : k + 8] * cosine
            coef_n[g * NF + k : g * NF + k + 8, :] = speed[k : k + 8] * sine

    sea = mask[...].astype(F32)
    sea_b = sea.astype(BF)
    before = (iota((LON, LON), 0) <= iota((LON, LON), 1)).astype(F32).astype(BF)
    rank = dot(sea_b, before)
    count = dot(sea_b, jnp.ones((LON, LON), BF))
    lower = (iota((ROWS, ROWS), 1) < iota((ROWS, ROWS), 0)).astype(F32).astype(BF)
    first = dot(lower, count.astype(BF))
    slot = first + rank - 1.0
    slot_mod = slot - LON * jnp.floor(slot * (1.0 / LON))
    place_at = jnp.where(sea > 0.5, slot_mod, -1.0)
    base = jnp.floor(first * (1.0 / LON))
    lane = iota((ROWS, LON), 1).astype(F32)
    window_at = base + jnp.where(lane < first - LON * base, 1.0, 0.0)
    for row in range(ROWS):
        slot_row[row] = place_at[row : row + 1]
        window_row[row] = window_at[row : row + 1]
        mask_row[row] = sea[row : row + 1]

    def build_row(row, carry):
        place = jnp.broadcast_to(slot_row[row], (LON, LON))
        which = iota((LON, LON), 0).astype(F32)
        onehot[row] = jnp.where(place == which, 1.0, 0.0).astype(BF)
        holds = jnp.broadcast_to(window_row[row], (STRIP, LON))
        for w in range(WINDOWS):
            windows[row, w] = jnp.where(holds == float(w), 1.0, 0.0).astype(BF)
        return carry

    lax.fori_loop(0, ROWS, build_row, 0)

    named = pattern[...]
    column = iota((ND, HALF), 1)
    chosen = jnp.zeros((ND, HALF), F32)
    for j in range(ND // 2):
        chosen = chosen + jnp.where(named[:, j : j + 1] == column, 1.0, 0.0)
    chosen = chosen.astype(BF)
    for g in range(GROUPS):
        wide = iota((HALF, SPEC * NF), 1)
        spread = (GROUPS * (wide // NF) + g == iota((HALF, SPEC * NF), 0)).astype(F32).astype(BF)
        wide_hits = dot(chosen, spread)
        for r in range(ND):
            hits[r, :, g * SPEC * NF : (g + 1) * SPEC * NF] = wide_hits[r : r + 1]

    left = (iota((NF, HALF), 0) == iota((NF, HALF), 1)).astype(F32).astype(BF)
    right = (iota((NF, HALF), 0) + NF == iota((NF, HALF), 1)).astype(F32).astype(BF)

    def build_pair(at, carry):
        m = at // SPEC
        s = lax.rem(at, SPEC)
        one = table[GROUPS * s + m]
        two = table[GROUPS * lax.rem(s + 1, SPEC) + m]
        pairs[at] = (dot(one, left) + dot(two, right)).astype(BF)
        return carry

    lax.fori_loop(0, GROUPS * SPEC, build_pair, 0)

    cur_up.wait()
    cur_down.wait()

    keep_south = jnp.where(tile > 0, 1.0, 0.0).astype(F32)
    keep_north = jnp.where(tile < TILES - 1, 1.0, 0.0).astype(F32)

    def propagate(comp):
        comps = pl.ds(comp, STRIP)
        lane_at = iota((STRIP, HALF), 1)
        first_lane = lane_at == 0
        last_lane = lane_at == HALF - 1
        a_e = coef_e[comps, :]
        a_n = coef_n[comps, :]

        def load(row):
            if row < 0:
                whole = halo[0, row + 2, comps, :].astype(F32) * keep_south
            elif row >= ROWS:
                whole = halo[1, row - ROWS, comps, :].astype(F32) * keep_north
            else:
                whole = action[row, comps, :].astype(F32)
            return whole[:, :HALF], whole[:, HALF:]

        def courant(row):
            e = current[row + 1, 0]
            n = current[row + 1, 1]
            res = []
            for h in range(2):
                cols = slice(h * HALF, (h + 1) * HALF)
                ce = a_e + jnp.concatenate([e[:, cols], e[:, cols]], axis=0)
                cn = a_n + jnp.concatenate([n[:, cols], n[:, cols]], axis=0)
                res.append((jnp.abs(ce), ce > 0.0, jnp.abs(cn), cn > 0.0))
            return res

        def update(south, here, north_of, speeds):
            lo, hi = here
            wl, wh = pltpu.roll(lo, 1, 1), pltpu.roll(hi, 1, 1)
            el, eh = pltpu.roll(lo, HALF - 1, 1), pltpu.roll(hi, HALF - 1, 1)
            west = (jnp.where(first_lane, 0.0, wl), jnp.where(first_lane, wl, wh))
            east_of = (jnp.where(last_lane, eh, el), jnp.where(last_lane, 0.0, eh))
            res = []
            for h in range(2):
                size_e, pos_e, size_n, pos_n = speeds[h]
                f = here[h]
                from_e = f - jnp.where(pos_e, west[h], east_of[h])
                from_n = f - jnp.where(pos_n, south[h], north_of[h])
                res.append(f - size_e * from_e - size_n * from_n)
            return tuple(res)

        f0 = {-2: load(-2), -1: load(-1)}
        f1 = {}
        speeds = {}
        for row in range(-1, ROWS + 1):
            f0[row + 1] = load(row + 1)
            speeds[row] = courant(row)
            f1[row] = update(f0[row - 1], f0[row], f0[row + 1], speeds[row])
            if row == -1:
                f1[row] = tuple(x * keep_south for x in f1[row])
            if row == ROWS:
                f1[row] = tuple(x * keep_north for x in f1[row])
            if row >= 1:
                done = update(f1[row - 2], f1[row - 1], f1[row], speeds[row - 1])
                moved[row - 1, comps, :] = jnp.concatenate(done, axis=1).astype(BF)

    def send_copy(g, peer):
        return pltpu.make_async_remote_copy(
            src_ref=send.at[g, peer], dst_ref=recv.at[g, me],
            send_sem=out_send.at[g], recv_sem=out_recv.at[g],
            device_id={"spec": peer}, device_id_type=MESH,
        )

    def back_copy(g, peer):
        return pltpu.make_async_remote_copy(
            src_ref=back_send.at[g, peer], dst_ref=back_recv.at[g, me],
            send_sem=ret_send.at[g], recv_sem=ret_recv.at[g],
            device_id={"spec": peer}, device_id_type=MESH,
        )

    def all_copies(src, dst, send_sem, recv_sem, g):
        others = pl.ds(0, SPEC - 1)
        return pltpu.make_async_remote_copy(
            src_ref=src.at[g, others], dst_ref=dst.at[g, others],
            send_sem=send_sem.at[g], recv_sem=recv_sem.at[g],
            device_id={"spec": lax.rem(me + 1, SPEC)}, device_id_type=MESH,
        )

    def outgoing(g, carry):
        to_up, to_down = halo_copies(g)
        to_up.wait()
        to_down.wait()
        comps = pl.ds(pl.multiple_of(g * NF, NF), NF)

        def strip(s, inner):
            propagate(pl.multiple_of(g * NF + s * STRIP, STRIP))
            return inner

        lax.fori_loop(0, NF // STRIP, strip, 0)

        def squeeze(row, inner):
            ring[row] = dot(moved[row, comps, :], onehot[row], 1, 1).astype(BF)
            return inner

        lax.fori_loop(0, ROWS, squeeze, 0)

        def gather(w, inner):
            for s in range(NF // STRIP):
                rows = slice(s * STRIP, (s + 1) * STRIP)
                packed = jnp.zeros((STRIP, LON), BF)
                for row in range(ROWS):
                    packed = packed + ring[row, rows, :] * windows[row, w]
                send[g, 2 * w, rows, :] = packed[:, :HALF]
                send[g, 2 * w + 1, rows, :] = packed[:, HALF:]
            return inner

        lax.fori_loop(0, WINDOWS, gather, 0)

        def start(i, inner):
            send_copy(g, lax.rem(me + i, SPEC)).start()
            return inner

        lax.fori_loop(1, SPEC, start, 0)
        recv[g, me] = send[g, me]
        return carry

    lax.fori_loop(0, GROUPS, outgoing, 0)

    def build_weight(at, carry):
        g = at // (GROUPS * SPEC)
        h = lax.rem(at // SPEC, GROUPS)
        q = lax.rem(at, SPEC)
        m = lax.rem(g - h + GROUPS, GROUPS)
        carried = (m + h - g) // GROUPS
        for i in range(SPEC // 2):
            s = lax.rem(2 * i - q - carried + 2 * SPEC, SPEC)
            col = pl.multiple_of(g * SPEC * NF + i * HALF, HALF)
            held = hits[GROUPS * q + h, :, pl.ds(col, HALF)]
            held = jnp.broadcast_to(held, (NF, HALF)).astype(BF)
            weight[g * GROUPS + h, pl.ds(pl.multiple_of(q * NF, NF), NF), i * HALF : (i + 1) * HALF] = (
                pairs[m * SPEC + s] * held
            )
        return carry

    lax.fori_loop(0, GROUPS * GROUPS * SPEC, build_weight, 0)

    for g in range(GROUPS):
        all_copies(send, recv, out_send, out_recv, g).wait_recv()

        def couple(h, carry, g=g):
            cells = recv[g].reshape(SPEC * NF, HALF)
            part = dot(weight[g * GROUPS + h], cells)
            if g == 0:
                total[h] = part
            elif g < GROUPS - 1:
                total[h] = total[h] + part
            else:
                coupled = total[h] + part
                own = recv[h].reshape(SPEC * NF, HALF).astype(F32)
                renewed = (own + own * coupled).astype(BF)
                back_send[h] = renewed.reshape(SPEC, NF, HALF)

                def start(i, inner):
                    back_copy(h, lax.rem(me + i, SPEC)).start()
                    return inner

                lax.fori_loop(1, SPEC, start, 0)
                back_recv[h, me] = back_send[h, me]
            return carry

        lax.fori_loop(0, GROUPS, couple, 0)

    def incoming(h, carry):
        all_copies(back_send, back_recv, ret_send, ret_recv, h).wait_recv()
        comps = pl.ds(pl.multiple_of(h * NF, NF), NF)

        def spread(row, inner):
            for s in range(NF // STRIP):
                rows = slice(s * STRIP, (s + 1) * STRIP)
                for half in range(2):
                    cols = slice(half * HALF, (half + 1) * HALF)
                    picked = jnp.zeros((STRIP, HALF), BF)
                    for w in range(WINDOWS):
                        picked = picked + back_recv[h, 2 * w + half, rows, :] * windows[row, w, :, cols]
                    ring[row, rows, cols] = picked
            wide = dot(ring[row], onehot[row], 1, 0)
            at_sea = jnp.broadcast_to(mask_row[row], (NF, LON)) > 0.5
            result = jnp.where(at_sea, wide, moved[row, comps, :].astype(F32))
            out[row, comps, :] = result.astype(BF)
            return inner

        lax.fori_loop(0, ROWS, spread, 0)
        return carry

    lax.fori_loop(0, GROUPS, incoming, 0)

    def finish(g, carry):
        all_copies(send, recv, out_send, out_recv, g).wait_send()
        all_copies(back_send, back_recv, ret_send, ret_recv, g).wait_send()
        return carry

    lax.fori_loop(0, GROUPS, finish, 0)


def local(action, east_current, north_current, sea_mask, pattern, table):
    vmem = pl.BlockSpec(memory_space=pltpu.VMEM)
    dma = pltpu.SemaphoreType.DMA
    comps = GROUPS * NF
    return pl.pallas_call(
        step_kernel,
        out_shape=jax.ShapeDtypeStruct((ROWS, comps, LON), BF),
        in_specs=[vmem] * 6,
        out_specs=vmem,
        scratch_shapes=[
            pltpu.VMEM((2, 2, comps, LON), BF),
            pltpu.VMEM((ROWS + 2, 2, 8, LON), F32),
            pltpu.VMEM((comps, HALF), F32),
            pltpu.VMEM((comps, HALF), F32),
            pltpu.VMEM((ROWS, comps, LON), BF),
            pltpu.VMEM((ROWS, 1, LON), F32),
            pltpu.VMEM((ROWS, 1, LON), F32),
            pltpu.VMEM((ROWS, 1, LON), F32),
            pltpu.VMEM((ROWS, LON, LON), BF),
            pltpu.VMEM((ROWS, WINDOWS, STRIP, LON), BF),
            pltpu.VMEM((ROWS, NF, LON), BF),
            pltpu.VMEM((GROUPS, SPEC, NF, HALF), BF),
            pltpu.VMEM((GROUPS, SPEC, NF, HALF), BF),
            pltpu.VMEM((GROUPS, SPEC * NF, HALF), F32),
            pltpu.VMEM((GROUPS * GROUPS, SPEC * NF, SPEC * NF), BF),
            pltpu.VMEM((GROUPS * SPEC, NF, HALF), BF),
            pltpu.VMEM((ND, 1, ND * NF), F32),
            pltpu.VMEM((GROUPS, SPEC, NF, HALF), BF),
            pltpu.VMEM((GROUPS, SPEC, NF, HALF), BF),
            dma((2, GROUPS)),
            dma((2, GROUPS)),
            dma((2,)),
            dma((2,)),
            dma((GROUPS,)),
            dma((GROUPS,)),
            dma((GROUPS,)),
            dma((GROUPS,)),
        ],
        compiler_params=pltpu.CompilerParams(
            collective_id=0, has_side_effects=True, vmem_limit_bytes=52 * 1024 * 1024
        ),
    )(action, east_current, north_current, sea_mask, pattern, table)


def solution(mesh):
    return jax.shard_map(
        local,
        mesh=mesh,
        in_specs=(
            P("tile", "spec", None),
            P("tile", None),
            P("tile", None),
            P("tile", None),
            P(),
            P(),
        ),
        out_specs=P("tile", "spec", None),
        check_vma=False,
    )
```

```python
import functools
import math

import jax
import jax.numpy as jnp
from jax import lax
from jax.experimental import pallas as pl
from jax.experimental.pallas import tpu as pltpu
from jax.sharding import PartitionSpec as P

NF = 64
ND = 48
GROUPS = 3
SPEC = 16
TILES = 32
ROWS = 16
LON = 256
HALF = 128
WINDOWS = 8
STRIP = 16
COURANT = 0.45
MESH = pl.DeviceIdType.MESH
BF = jnp.bfloat16
F32 = jnp.float32


def iota(shape, dim):
    return lax.broadcasted_iota(jnp.int32, shape, dim)


def dot(a, b, ca=1, cb=0):
    return lax.dot_general(a, b, (((ca,), (cb,)), ((), ())), preferred_element_type=F32)


def step_kernel(
    action_hbm, east_hbm, north_hbm, mask_hbm, pattern_hbm, table_hbm, out_hbm, moved_hbm,
    action, east, north, mask, pattern, table, out, halo, current, coef_e, coef_n, moved, slot_row, window_row, onehot, windows, ring,
    send, recv, total, weight, pairs, hits, back_send, back_recv,
    halo_send, halo_recv, cur_send, cur_recv, out_send, out_recv, ret_send, ret_recv,
    load_sem, action_sem, store_sem, moved_sem,
):
    me = lax.axis_index("spec")
    tile = lax.axis_index("tile")
    up = lax.rem(tile + 1, TILES)
    down = lax.rem(tile + TILES - 1, TILES)

    small = [
        pltpu.make_async_copy(src, dst, load_sem.at[i])
        for i, (src, dst) in enumerate(
            ((east_hbm, east), (north_hbm, north), (mask_hbm, mask), (pattern_hbm, pattern), (table_hbm, table))
        )
    ]
    for copy in small:
        copy.start()

    def group(g):
        return pl.ds(pl.multiple_of(g * NF, NF), NF)

    def action_copy(g):
        return pltpu.make_async_copy(
            action_hbm.at[:, group(g)], action.at[:, group(g)], action_sem.at[g]
        )

    for g in range(GROUPS):
        action_copy(g).start()

    barrier = pltpu.get_barrier_semaphore()

    def greet(i, carry):
        pl.semaphore_signal(
            barrier, inc=1, device_id={"spec": lax.rem(me + i, SPEC)}, device_id_type=MESH
        )
        return carry

    lax.fori_loop(1, SPEC, greet, 0)
    pl.semaphore_signal(barrier, inc=1, device_id={"tile": up}, device_id_type=MESH)
    pl.semaphore_signal(barrier, inc=1, device_id={"tile": down}, device_id_type=MESH)

    small[0].wait()
    small[1].wait()

    for row in range(ROWS):
        current[row + 1, 0] = jnp.broadcast_to(COURANT * east[row : row + 1, :], (8, LON))
        current[row + 1, 1] = jnp.broadcast_to(COURANT * north[row : row + 1, :], (8, LON))

    pl.semaphore_wait(barrier, SPEC + 1)

    cur_up = pltpu.make_async_remote_copy(
        src_ref=current.at[ROWS], dst_ref=current.at[0],
        send_sem=cur_send.at[0], recv_sem=cur_recv.at[0],
        device_id={"tile": up}, device_id_type=MESH,
    )
    cur_down = pltpu.make_async_remote_copy(
        src_ref=current.at[1], dst_ref=current.at[ROWS + 1],
        send_sem=cur_send.at[1], recv_sem=cur_recv.at[1],
        device_id={"tile": down}, device_id_type=MESH,
    )
    cur_up.start()
    cur_down.start()

    def halo_copies(g):
        comps = group(g)
        to_up = pltpu.make_async_remote_copy(
            src_ref=action_hbm.at[pl.ds(ROWS - 2, 2), comps], dst_ref=halo.at[0, :, comps],
            send_sem=halo_send.at[0, g], recv_sem=halo_recv.at[0, g],
            device_id={"tile": up}, device_id_type=MESH,
        )
        to_down = pltpu.make_async_remote_copy(
            src_ref=action_hbm.at[pl.ds(0, 2), comps], dst_ref=halo.at[1, :, comps],
            send_sem=halo_send.at[1, g], recv_sem=halo_recv.at[1, g],
            device_id={"tile": down}, device_id_type=MESH,
        )
        return to_up, to_down

    def start_halo(g, carry):
        to_up, to_down = halo_copies(g)
        to_up.start()
        to_down.start()
        return carry

    lax.fori_loop(0, GROUPS, start_halo, 0)

    speed = jnp.exp(iota((NF, HALF), 0).astype(F32) * (-2.0 / (NF - 1)))
    for g in range(GROUPS):
        direction = jnp.full((8, HALF), me * GROUPS + g, jnp.int32).astype(F32)
        theta = direction * (2.0 * math.pi / ND)
        cosine = COURANT * jnp.cos(theta)
        sine = COURANT * jnp.sin(theta)
        for k in range(0, NF, 8):
            coef_e[g * NF + k : g * NF + k + 8, :] = speed[k : k + 8] * cosine
            coef_n[g * NF + k : g * NF + k + 8, :] = speed[k : k + 8] * sine

    small[2].wait()
    sea = mask[...].astype(F32)
    sea_b = sea.astype(BF)
    before = (iota((LON, LON), 0) <= iota((LON, LON), 1)).astype(F32).astype(BF)
    rank = dot(sea_b, before)
    count = dot(sea_b, jnp.ones((LON, LON), BF))
    lower = (iota((ROWS, ROWS), 1) < iota((ROWS, ROWS), 0)).astype(F32).astype(BF)
    first = dot(lower, count.astype(BF))
    slot = first + rank - 1.0
    slot_mod = slot - LON * jnp.floor(slot * (1.0 / LON))
    place_at = jnp.where(sea > 0.5, slot_mod, -1.0)
    base = jnp.floor(first * (1.0 / LON))
    lane = iota((ROWS, LON), 1).astype(F32)
    window_at = base + jnp.where(lane < first - LON * base, 1.0, 0.0)
    for row in range(ROWS):
        slot_row[row] = place_at[row : row + 1]
        window_row[row] = window_at[row : row + 1]

    def build_row(row, carry):
        place = jnp.broadcast_to(slot_row[row], (LON, LON))
        which = iota((LON, LON), 0).astype(F32)
        onehot[row] = jnp.where(place == which, 1.0, 0.0).astype(BF)
        holds = jnp.broadcast_to(window_row[row], (STRIP, LON))
        for w in range(WINDOWS):
            windows[row, w] = jnp.where(holds == float(w), 1.0, 0.0).astype(BF)
        return carry

    lax.fori_loop(0, ROWS, build_row, 0)

    small[3].wait()
    column = iota((HALF, ND), 0)
    chosen = jnp.zeros((HALF, ND), F32)
    for j in range(ND // 2):
        named = jnp.broadcast_to(pattern[j : j + 1, :], (HALF, ND))
        chosen = chosen + jnp.where(named == column, 1.0, 0.0)
    chosen = chosen.astype(BF)
    for g in range(GROUPS):
        wide = iota((HALF, SPEC * NF), 1)
        spread = (GROUPS * (wide // NF) + g == iota((HALF, SPEC * NF), 0)).astype(F32).astype(BF)
        wide_hits = dot(chosen, spread, 0, 0)
        for r in range(ND):
            hits[r, :, g * SPEC * NF : (g + 1) * SPEC * NF] = wide_hits[r : r + 1]

    small[4].wait()

    def build_pair(s, carry):
        for m in range(GROUPS):
            one = table[GROUPS * s + m]
            two = table[GROUPS * lax.rem(s + 1, SPEC) + m]
            pair = jnp.concatenate([one, two], axis=1)
            pairs[m * 2 * SPEC + s] = pair
            pairs[m * 2 * SPEC + SPEC + s] = pair
        return carry

    lax.fori_loop(0, SPEC, build_pair, 0)

    cur_up.wait()
    cur_down.wait()

    keep_south = jnp.where(tile > 0, 1.0, 0.0).astype(F32)
    keep_north = jnp.where(tile < TILES - 1, 1.0, 0.0).astype(F32)

    def propagate(comp):
        comps = pl.ds(comp, STRIP)
        lane_at = iota((STRIP, HALF), 1)
        first_lane = lane_at == 0
        last_lane = lane_at == HALF - 1
        a_e = coef_e[comps, :]
        a_n = coef_n[comps, :]

        def load(row):
            if row < 0:
                whole = halo[0, row + 2, comps, :].astype(F32) * keep_south
            elif row >= ROWS:
                whole = halo[1, row - ROWS, comps, :].astype(F32) * keep_north
            else:
                whole = action[row, comps, :].astype(F32)
            return whole[:, :HALF], whole[:, HALF:]

        def courant(row):
            e = current[row + 1, 0]
            n = current[row + 1, 1]
            res = []
            for h in range(2):
                cols = slice(h * HALF, (h + 1) * HALF)
                ce = a_e + jnp.concatenate([e[:, cols], e[:, cols]], axis=0)
                cn = a_n + jnp.concatenate([n[:, cols], n[:, cols]], axis=0)
                res.append((jnp.abs(ce), ce > 0.0, jnp.abs(cn), cn > 0.0))
            return res

        def update(south, here, north_of, speeds):
            lo, hi = here
            wl, wh = pltpu.roll(lo, 1, 1), pltpu.roll(hi, 1, 1)
            el, eh = pltpu.roll(lo, HALF - 1, 1), pltpu.roll(hi, HALF - 1, 1)
            west = (jnp.where(first_lane, 0.0, wl), jnp.where(first_lane, wl, wh))
            east_of = (jnp.where(last_lane, eh, el), jnp.where(last_lane, 0.0, eh))
            res = []
            for h in range(2):
                size_e, pos_e, size_n, pos_n = speeds[h]
                f = here[h]
                from_e = f - jnp.where(pos_e, west[h], east_of[h])
                from_n = f - jnp.where(pos_n, south[h], north_of[h])
                res.append(f - size_e * from_e - size_n * from_n)
            return tuple(res)

        f0 = {-2: load(-2), -1: load(-1)}
        f1 = {}
        speeds = {}
        for row in range(-1, ROWS + 1):
            f0[row + 1] = load(row + 1)
            speeds[row] = courant(row)
            f1[row] = update(f0[row - 1], f0[row], f0[row + 1], speeds[row])
            if row == -1:
                f1[row] = tuple(x * keep_south for x in f1[row])
            if row == ROWS:
                f1[row] = tuple(x * keep_north for x in f1[row])
            if row >= 1:
                done = update(f1[row - 2], f1[row - 1], f1[row], speeds[row - 1])
                moved[row - 1, comps, :] = jnp.concatenate(done, axis=1).astype(BF)

    def moved_copy(g):
        return pltpu.make_async_copy(
            moved.at[:, group(g)], moved_hbm.at[:, group(g)], moved_sem.at[g]
        )

    def send_copy(g, peer):
        return pltpu.make_async_remote_copy(
            src_ref=send.at[g, peer], dst_ref=recv.at[g, me],
            send_sem=out_send.at[g], recv_sem=out_recv.at[g],
            device_id={"spec": peer}, device_id_type=MESH,
        )

    def back_copy(g, peer):
        return pltpu.make_async_remote_copy(
            src_ref=back_send.at[g, peer], dst_ref=back_recv.at[g, me],
            send_sem=ret_send.at[g], recv_sem=ret_recv.at[g],
            device_id={"spec": peer}, device_id_type=MESH,
        )

    def all_copies(src, dst, send_sem, recv_sem, g):
        others = pl.ds(0, SPEC - 1)
        return pltpu.make_async_remote_copy(
            src_ref=src.at[g, others], dst_ref=dst.at[g, others],
            send_sem=send_sem.at[g], recv_sem=recv_sem.at[g],
            device_id={"spec": lax.rem(me + 1, SPEC)}, device_id_type=MESH,
        )

    def outgoing(g, carry):
        to_up, to_down = halo_copies(g)
        action_copy(g).wait()
        to_up.wait()
        to_down.wait()
        comps = group(g)

        def strip(s, inner):
            propagate(pl.multiple_of(g * NF + s * STRIP, STRIP))
            return inner

        lax.fori_loop(0, NF // STRIP, strip, 0)

        moved_copy(g).start()
        for row in range(ROWS):
            ring[row] = dot(moved[row, comps, :], onehot[row], 1, 1).astype(BF)

        def gather(w, inner):
            for s in range(NF // STRIP):
                rows = slice(s * STRIP, (s + 1) * STRIP)
                packed = jnp.zeros((STRIP, LON), BF)
                for row in range(ROWS):
                    packed = packed + ring[row, rows, :] * windows[row, w]
                send[g, 2 * w, rows, :] = packed[:, :HALF]
                send[g, 2 * w + 1, rows, :] = packed[:, HALF:]
            return inner

        lax.fori_loop(0, WINDOWS, gather, 0)

        def start(i, inner):
            send_copy(g, lax.rem(me + i, SPEC)).start()
            return inner

        lax.fori_loop(1, SPEC, start, 0)
        recv[g, me] = send[g, me]
        return carry

    lax.fori_loop(0, GROUPS, outgoing, 0)

    for g in range(GROUPS):
        for h in range(GROUPS):
            m = (g - h) % GROUPS
            carried = (m + h - g) // GROUPS

            def build_weight(q, carry, g=g, h=h, m=m, carried=carried):
                at = m * 2 * SPEC + SPEC - carried - q
                for i in range(SPEC // 2):
                    col = g * SPEC * NF + i * HALF
                    held = hits[GROUPS * q + h, :, col : col + HALF]
                    held = jnp.broadcast_to(held, (STRIP, HALF)).astype(BF)
                    for k in range(0, NF, STRIP):
                        weight[
                            g * GROUPS + h,
                            pl.ds(pl.multiple_of(q * NF + k, STRIP), STRIP),
                            i * HALF : (i + 1) * HALF,
                        ] = pairs[at + 2 * i, k : k + STRIP, :] * held
                return carry

            lax.fori_loop(0, SPEC, build_weight, 0)

    for g in range(GROUPS):
        all_copies(send, recv, out_send, out_recv, g).wait_recv()

        def couple(h, carry, g=g):
            cells = recv[g].reshape(SPEC * NF, HALF)
            part = dot(weight[g * GROUPS + h], cells)
            if g == 0:
                total[h] = part
            elif g < GROUPS - 1:
                total[h] = total[h] + part
            else:
                coupled = total[h] + part
                own = recv[h].reshape(SPEC * NF, HALF).astype(F32)
                renewed = (own + own * coupled).astype(BF)
                back_send[h] = renewed.reshape(SPEC, NF, HALF)

                def start(i, inner):
                    back_copy(h, lax.rem(me + i, SPEC)).start()
                    return inner

                lax.fori_loop(1, SPEC, start, 0)
                back_recv[h, me] = back_send[h, me]
            return carry

        lax.fori_loop(0, GROUPS, couple, 0)

    def out_copy(h):
        return pltpu.make_async_copy(out.at[:, group(h)], out_hbm.at[:, group(h)], store_sem.at[h])

    def incoming(h, carry):
        all_copies(back_send, back_recv, ret_send, ret_recv, h).wait_recv()
        comps = group(h)

        def pick(row, inner):
            for s in range(NF // STRIP):
                rows = slice(s * STRIP, (s + 1) * STRIP)
                for half in range(2):
                    cols = slice(half * HALF, (half + 1) * HALF)
                    picked = jnp.zeros((STRIP, HALF), BF)
                    for w in range(WINDOWS):
                        picked = picked + back_recv[h, 2 * w + half, rows, :] * windows[row, w, :, cols]
                    ring[row, rows, cols] = picked
            return inner

        lax.fori_loop(0, ROWS, pick, 0)
        for row in range(ROWS):
            out[row, comps, :] = dot(ring[row], onehot[row], 1, 0).astype(BF)
        out_copy(h).start()
        return carry

    lax.fori_loop(0, GROUPS, incoming, 0)

    def finish(g, carry):
        all_copies(send, recv, out_send, out_recv, g).wait_send()
        all_copies(back_send, back_recv, ret_send, ret_recv, g).wait_send()
        out_copy(g).wait()
        moved_copy(g).wait()
        return carry

    lax.fori_loop(0, GROUPS, finish, 0)


def local(action, east_current, north_current, sea_mask, pattern, table):
    hbm = pl.BlockSpec(memory_space=pltpu.HBM)
    dma = pltpu.SemaphoreType.DMA
    comps = GROUPS * NF
    renewed, moved = pl.pallas_call(
        step_kernel,
        out_shape=[jax.ShapeDtypeStruct((ROWS, comps, LON), BF)] * 2,
        in_specs=[hbm] * 6,
        out_specs=[hbm] * 2,
        scratch_shapes=[
            pltpu.VMEM((ROWS, comps, LON), BF),
            pltpu.VMEM((ROWS, LON), F32),
            pltpu.VMEM((ROWS, LON), F32),
            pltpu.VMEM((ROWS, LON), jnp.int32),
            pltpu.VMEM((ND // 2, ND), jnp.int32),
            pltpu.VMEM((ND, NF, NF), BF),
            pltpu.VMEM((ROWS, comps, LON), BF),
            pltpu.VMEM((2, 2, comps, LON), BF),
            pltpu.VMEM((ROWS + 2, 2, 8, LON), F32),
            pltpu.VMEM((comps, HALF), F32),
            pltpu.VMEM((comps, HALF), F32),
            pltpu.VMEM((ROWS, comps, LON), BF),
            pltpu.VMEM((ROWS, 1, LON), F32),
            pltpu.VMEM((ROWS, 1, LON), F32),
            pltpu.VMEM((ROWS, LON, LON), BF),
            pltpu.VMEM((ROWS, WINDOWS, STRIP, LON), BF),
            pltpu.VMEM((ROWS, NF, LON), BF),
            pltpu.VMEM((GROUPS, SPEC, NF, HALF), BF),
            pltpu.VMEM((GROUPS, SPEC, NF, HALF), BF),
            pltpu.VMEM((GROUPS, SPEC * NF, HALF), F32),
            pltpu.VMEM((GROUPS * GROUPS, SPEC * NF, SPEC * NF), BF),
            pltpu.VMEM((GROUPS * 2 * SPEC, NF, HALF), BF),
            pltpu.VMEM((ND, 1, ND * NF), F32),
            pltpu.VMEM((GROUPS, SPEC, NF, HALF), BF),
            pltpu.VMEM((GROUPS, SPEC, NF, HALF), BF),
            dma((2, GROUPS)),
            dma((2, GROUPS)),
            dma((2,)),
            dma((2,)),
            dma((GROUPS,)),
            dma((GROUPS,)),
            dma((GROUPS,)),
            dma((GROUPS,)),
            dma((5,)),
            dma((GROUPS,)),
            dma((GROUPS,)),
            dma((GROUPS,)),
        ],
        compiler_params=pltpu.CompilerParams(
            collective_id=0, has_side_effects=True, vmem_limit_bytes=64 * 1024 * 1024
        ),
    )(action, east_current, north_current, sea_mask, pattern.T, table)
    return jnp.where(sea_mask[:, None, :] > 0, renewed, moved)


def solution(mesh):
    return jax.shard_map(
        local,
        mesh=mesh,
        in_specs=(
            P("tile", "spec", None),
            P("tile", None),
            P("tile", None),
            P("tile", None),
            P(),
            P(),
        ),
        out_specs=P("tile", "spec", None),
        check_vma=False,
    )
```

```python
import functools
import math

import jax
import jax.numpy as jnp
from jax import lax
from jax.experimental import pallas as pl
from jax.experimental.pallas import tpu as pltpu
from jax.sharding import PartitionSpec as P

NF = 64
ND = 48
GROUPS = 3
SPEC = 16
TILES = 32
ROWS = 16
LON = 256
HALF = 128
WINDOWS = 8
STRIP = 16
COURANT = 0.45
MESH = pl.DeviceIdType.MESH
BF = jnp.bfloat16
F32 = jnp.float32


def iota(shape, dim):
    return lax.broadcasted_iota(jnp.int32, shape, dim)


def dot(a, b, ca=1, cb=0):
    return lax.dot_general(a, b, (((ca,), (cb,)), ((), ())), preferred_element_type=F32)


def step_kernel(
    action_hbm, east_hbm, north_hbm, mask_hbm, pattern_hbm, table_hbm, out_hbm,
    action, east, north, mask, pattern, table, out, halo, current, coef_e, coef_n, moved, slot_row, window_row, mask_row, onehot, windows, ring,
    send, recv, total, weight_a, weight_b, pairs, hits, back_send, back_recv,
    halo_send, halo_recv, cur_send, cur_recv, out_send, out_recv, ret_send, ret_recv,
    load_sem, action_sem, store_sem,
):
    weight = (weight_a, weight_b)
    me = lax.axis_index("spec")
    tile = lax.axis_index("tile")
    up = lax.rem(tile + 1, TILES)
    down = lax.rem(tile + TILES - 1, TILES)

    barrier = pltpu.get_barrier_semaphore()

    pl.semaphore_signal(barrier, inc=1, device_id={"tile": up}, device_id_type=MESH)
    pl.semaphore_signal(barrier, inc=1, device_id={"tile": down}, device_id_type=MESH)

    def greet(i, carry):
        pl.semaphore_signal(
            barrier, inc=1, device_id={"spec": lax.rem(me + i, SPEC)}, device_id_type=MESH
        )
        return carry

    lax.fori_loop(1, SPEC, greet, 0)

    small = [
        pltpu.make_async_copy(src, dst, load_sem.at[i])
        for i, (src, dst) in enumerate(
            ((east_hbm, east), (north_hbm, north), (mask_hbm, mask), (pattern_hbm, pattern), (table_hbm, table))
        )
    ]
    for copy in small:
        copy.start()

    def group(g):
        return pl.ds(pl.multiple_of(g * NF, NF), NF)

    def action_copy(g):
        return pltpu.make_async_copy(
            action_hbm.at[:, group(g)], action.at[:, group(g)], action_sem.at[g]
        )

    for g in range(GROUPS):
        action_copy(g).start()


    small[0].wait()
    small[1].wait()

    for row in range(ROWS):
        current[row + 1, 0] = jnp.broadcast_to(COURANT * east[row : row + 1, :], (8, LON))
        current[row + 1, 1] = jnp.broadcast_to(COURANT * north[row : row + 1, :], (8, LON))

    pl.semaphore_wait(barrier, SPEC + 1)

    cur_up = pltpu.make_async_remote_copy(
        src_ref=current.at[ROWS], dst_ref=current.at[0],
        send_sem=cur_send.at[0], recv_sem=cur_recv.at[0],
        device_id={"tile": up}, device_id_type=MESH,
    )
    cur_down = pltpu.make_async_remote_copy(
        src_ref=current.at[1], dst_ref=current.at[ROWS + 1],
        send_sem=cur_send.at[1], recv_sem=cur_recv.at[1],
        device_id={"tile": down}, device_id_type=MESH,
    )
    cur_up.start()
    cur_down.start()

    def halo_copies(g):
        comps = group(g)
        to_up = pltpu.make_async_remote_copy(
            src_ref=action_hbm.at[pl.ds(ROWS - 2, 2), comps], dst_ref=halo.at[0, :, comps],
            send_sem=halo_send.at[0, g], recv_sem=halo_recv.at[0, g],
            device_id={"tile": up}, device_id_type=MESH,
        )
        to_down = pltpu.make_async_remote_copy(
            src_ref=action_hbm.at[pl.ds(0, 2), comps], dst_ref=halo.at[1, :, comps],
            send_sem=halo_send.at[1, g], recv_sem=halo_recv.at[1, g],
            device_id={"tile": down}, device_id_type=MESH,
        )
        return to_up, to_down

    def start_halo(g, carry):
        to_up, to_down = halo_copies(g)
        to_up.start()
        to_down.start()
        return carry

    lax.fori_loop(0, GROUPS, start_halo, 0)

    speed = jnp.exp(iota((NF, HALF), 0).astype(F32) * (-2.0 / (NF - 1)))
    for g in range(GROUPS):
        direction = jnp.full((8, HALF), me * GROUPS + g, jnp.int32).astype(F32)
        theta = direction * (2.0 * math.pi / ND)
        cosine = COURANT * jnp.cos(theta)
        sine = COURANT * jnp.sin(theta)
        for k in range(0, NF, 8):
            coef_e[g * NF + k : g * NF + k + 8, :] = speed[k : k + 8] * cosine
            coef_n[g * NF + k : g * NF + k + 8, :] = speed[k : k + 8] * sine

    small[2].wait()
    sea = mask[...].astype(F32)
    sea_b = sea.astype(BF)
    before = (iota((LON, LON), 0) <= iota((LON, LON), 1)).astype(F32).astype(BF)
    rank = dot(sea_b, before)
    count = dot(sea_b, jnp.ones((LON, LON), BF))
    lower = (iota((ROWS, ROWS), 1) < iota((ROWS, ROWS), 0)).astype(F32).astype(BF)
    first = dot(lower, count.astype(BF))
    slot = first + rank - 1.0
    slot_mod = slot - LON * jnp.floor(slot * (1.0 / LON))
    place_at = jnp.where(sea > 0.5, slot_mod, -1.0)
    base = jnp.floor(first * (1.0 / LON))
    lane = iota((ROWS, LON), 1).astype(F32)
    window_at = base + jnp.where(lane < first - LON * base, 1.0, 0.0)
    for row in range(ROWS):
        slot_row[row] = place_at[row : row + 1]
        window_row[row] = window_at[row : row + 1]
        mask_row[row] = sea[row : row + 1]

    def build_row(row, carry):
        place = jnp.broadcast_to(slot_row[row], (LON, LON))
        which = iota((LON, LON), 0).astype(F32)
        onehot[row] = jnp.where(place == which, 1.0, 0.0).astype(BF)
        holds = jnp.broadcast_to(window_row[row], (STRIP, LON))
        for w in range(WINDOWS):
            windows[row, w] = jnp.where(holds == float(w), 1.0, 0.0).astype(BF)
        return carry

    lax.fori_loop(0, ROWS, build_row, 0)

    small[3].wait()
    column = iota((HALF, ND), 0)
    chosen = jnp.zeros((HALF, ND), F32)
    for j in range(ND // 2):
        named = jnp.broadcast_to(pattern[j : j + 1, :], (HALF, ND))
        chosen = chosen + jnp.where(named == column, 1.0, 0.0)
    chosen = chosen.astype(BF)
    for g in range(GROUPS):
        wide = iota((HALF, SPEC * NF), 1)
        spread = (GROUPS * (wide // NF) + g == iota((HALF, SPEC * NF), 0)).astype(F32).astype(BF)
        wide_hits = dot(chosen, spread, 0, 0)
        for r in range(ND):
            hits[r, :, g * SPEC * NF : (g + 1) * SPEC * NF] = wide_hits[r : r + 1]

    small[4].wait()

    def build_pair(s, carry):
        for m in range(GROUPS):
            one = table[GROUPS * s + m]
            two = table[GROUPS * lax.rem(s + 1, SPEC) + m]
            pair = jnp.concatenate([one, two], axis=1)
            pairs[m * 2 * SPEC + s] = pair
            pairs[m * 2 * SPEC + SPEC + s] = pair
        return carry

    lax.fori_loop(0, SPEC, build_pair, 0)

    cur_up.wait()
    cur_down.wait()

    keep_south = jnp.where(tile > 0, 1.0, 0.0).astype(F32)
    keep_north = jnp.where(tile < TILES - 1, 1.0, 0.0).astype(F32)

    def propagate(comp):
        comps = pl.ds(comp, STRIP)
        lane_at = iota((STRIP, HALF), 1)
        first_lane = lane_at == 0
        last_lane = lane_at == HALF - 1
        a_e = coef_e[comps, :]
        a_n = coef_n[comps, :]

        def load(row):
            if row < 0:
                whole = halo[0, row + 2, comps, :] * keep_south.astype(BF)
            elif row >= ROWS:
                whole = halo[1, row - ROWS, comps, :] * keep_north.astype(BF)
            else:
                whole = action[row, comps, :]
            return whole[:, :HALF], whole[:, HALF:]

        def wide(pair):
            return tuple(x.astype(F32) for x in pair)

        def courant(row):
            e = current[row + 1, 0]
            n = current[row + 1, 1]
            res = []
            for h in range(2):
                cols = slice(h * HALF, (h + 1) * HALF)
                ce = a_e + jnp.concatenate([e[:, cols], e[:, cols]], axis=0)
                cn = a_n + jnp.concatenate([n[:, cols], n[:, cols]], axis=0)
                res.append((jnp.abs(ce), ce > 0.0, jnp.abs(cn), cn > 0.0))
            return res

        def turn(pair, shift):
            return tuple(pltpu.roll(x, shift, 1).astype(F32) for x in pair)

        def update(south, here, north_of, speeds, narrow=None):
            wl, wh = turn(narrow or here, 1)
            el, eh = turn(narrow or here, HALF - 1)
            west = (jnp.where(first_lane, 0.0, wl), jnp.where(first_lane, wl, wh))
            east_of = (jnp.where(last_lane, eh, el), jnp.where(last_lane, 0.0, eh))
            res = []
            for h in range(2):
                size_e, pos_e, size_n, pos_n = speeds[h]
                f = here[h]
                from_e = f - jnp.where(pos_e, west[h], east_of[h])
                from_n = f - jnp.where(pos_n, south[h], north_of[h])
                res.append(f - size_e * from_e - size_n * from_n)
            return tuple(res)

        raw = {-2: load(-2), -1: load(-1)}
        f0 = {-2: wide(raw[-2]), -1: wide(raw[-1])}
        f1 = {}
        speeds = {}
        for row in range(-1, ROWS + 1):
            raw[row + 1] = load(row + 1)
            f0[row + 1] = wide(raw[row + 1])
            speeds[row] = courant(row)
            f1[row] = update(f0[row - 1], f0[row], f0[row + 1], speeds[row], raw[row])
            if row == -1:
                f1[row] = tuple(x * keep_south for x in f1[row])
            if row == ROWS:
                f1[row] = tuple(x * keep_north for x in f1[row])
            if row >= 1:
                done = update(f1[row - 2], f1[row - 1], f1[row], speeds[row - 1])
                moved[row - 1, comps, :] = jnp.concatenate(done, axis=1).astype(BF)

    def send_copy(g, peer):
        return pltpu.make_async_remote_copy(
            src_ref=send.at[g, peer], dst_ref=recv.at[g, me],
            send_sem=out_send.at[g], recv_sem=out_recv.at[g],
            device_id={"spec": peer}, device_id_type=MESH,
        )

    def back_copy(g, peer):
        return pltpu.make_async_remote_copy(
            src_ref=back_send.at[g, peer], dst_ref=back_recv.at[g, me],
            send_sem=ret_send.at[g], recv_sem=ret_recv.at[g],
            device_id={"spec": peer}, device_id_type=MESH,
        )

    def all_copies(src, dst, send_sem, recv_sem, g):
        others = pl.ds(0, SPEC - 1)
        return pltpu.make_async_remote_copy(
            src_ref=src.at[g, others], dst_ref=dst.at[g, others],
            send_sem=send_sem.at[g], recv_sem=recv_sem.at[g],
            device_id={"spec": lax.rem(me + 1, SPEC)}, device_id_type=MESH,
        )

    def outgoing(g):
        to_up, to_down = halo_copies(g)
        action_copy(g).wait()
        to_up.wait()
        to_down.wait()
        comps = group(g)

        def strip(s, inner):
            propagate(pl.multiple_of(g * NF + s * STRIP, STRIP))
            return inner

        lax.fori_loop(0, NF // STRIP, strip, 0)

        for row in range(ROWS):
            ring[row] = dot(moved[row, comps, :], onehot[row], 1, 1).astype(BF)

        def gather(w, inner):
            for s in range(NF // STRIP):
                rows = slice(s * STRIP, (s + 1) * STRIP)
                packed = jnp.zeros((STRIP, LON), BF)
                for row in range(ROWS):
                    packed = packed + ring[row, rows, :] * windows[row, w]
                send[g, 2 * w, rows, :] = packed[:, :HALF]
                send[g, 2 * w + 1, rows, :] = packed[:, HALF:]
            return inner

        lax.fori_loop(0, WINDOWS, gather, 0)

        def start(i, inner):
            send_copy(g, lax.rem(me + i, SPEC)).start()
            return inner

        lax.fori_loop(1, SPEC, start, 0)
        recv[g, me] = send[g, me]

    def build_weight(at, q):
        g, h = divmod(at, GROUPS)
        m = (g - h) % GROUPS
        first_pair = m * 2 * SPEC + SPEC - (m + h - g) // GROUPS - q
        for i in range(SPEC // 2):
            col = g * SPEC * NF + i * HALF
            held = hits[GROUPS * q + h, :, col : col + HALF]
            held = jnp.broadcast_to(held, (STRIP, HALF)).astype(BF)
            for k in range(0, NF, STRIP):
                weight[at % 2][q * NF + k : q * NF + k + STRIP, i * HALF : (i + 1) * HALF] = (
                    pairs[first_pair + 2 * i, k : k + STRIP, :] * held
                )

    def couple(g):
        all_copies(send, recv, out_send, out_recv, g).wait_recv()
        cells = recv[g].reshape(SPEC * NF, HALF)
        for h in range(GROUPS):
            at = g * GROUPS + h
            part = dot(weight[at % 2][...], cells)
            if at + 1 < GROUPS * GROUPS:
                for q in range(SPEC):
                    build_weight(at + 1, q)
            if g == 0:
                total[h] = part
            elif g < GROUPS - 1:
                total[h] = total[h] + part
            else:
                coupled = total[h] + part
                own = recv[h].reshape(SPEC * NF, HALF).astype(F32)
                renewed = (own + own * coupled).astype(BF)
                back_send[h] = renewed.reshape(SPEC, NF, HALF)

                def start(i, inner, h=h):
                    back_copy(h, lax.rem(me + i, SPEC)).start()
                    return inner

                lax.fori_loop(1, SPEC, start, 0)
                back_recv[h, me] = back_send[h, me]

    for q in range(SPEC):
        build_weight(0, q)
    outgoing(0)
    outgoing(1)
    couple(0)
    outgoing(2)
    couple(1)
    couple(2)

    def out_copy(h):
        return pltpu.make_async_copy(out.at[:, group(h)], out_hbm.at[:, group(h)], store_sem.at[h])

    def incoming(h, carry):
        all_copies(back_send, back_recv, ret_send, ret_recv, h).wait_recv()
        comps = group(h)

        def pick(row, inner):
            for s in range(NF // STRIP):
                rows = slice(s * STRIP, (s + 1) * STRIP)
                for half in range(2):
                    cols = slice(half * HALF, (half + 1) * HALF)
                    picked = jnp.zeros((STRIP, HALF), BF)
                    for w in range(WINDOWS):
                        picked = picked + back_recv[h, 2 * w + half, rows, :] * windows[row, w, :, cols]
                    ring[row, rows, cols] = picked
            return inner

        lax.fori_loop(0, ROWS, pick, 0)
        for row in range(ROWS):
            wide = dot(ring[row], onehot[row], 1, 0)
            at_sea = jnp.broadcast_to(mask_row[row], (NF, LON)) > 0.5
            result = jnp.where(at_sea, wide, moved[row, comps, :].astype(F32))
            out[row, comps, :] = result.astype(BF)
        out_copy(h).start()
        return carry

    lax.fori_loop(0, GROUPS, incoming, 0)

    def finish(g, carry):
        all_copies(send, recv, out_send, out_recv, g).wait_send()
        all_copies(back_send, back_recv, ret_send, ret_recv, g).wait_send()
        out_copy(g).wait()
        return carry

    lax.fori_loop(0, GROUPS, finish, 0)


def local(action, east_current, north_current, sea_mask, pattern, table):
    hbm = pl.BlockSpec(memory_space=pltpu.HBM)
    dma = pltpu.SemaphoreType.DMA
    comps = GROUPS * NF
    return pl.pallas_call(
        step_kernel,
        out_shape=jax.ShapeDtypeStruct((ROWS, comps, LON), BF),
        in_specs=[hbm] * 6,
        out_specs=hbm,
        scratch_shapes=[
            pltpu.VMEM((ROWS, comps, LON), BF),
            pltpu.VMEM((ROWS, LON), F32),
            pltpu.VMEM((ROWS, LON), F32),
            pltpu.VMEM((ROWS, LON), jnp.int32),
            pltpu.VMEM((ND // 2, ND), jnp.int32),
            pltpu.VMEM((ND, NF, NF), BF),
            pltpu.VMEM((ROWS, comps, LON), BF),
            pltpu.VMEM((2, 2, comps, LON), BF),
            pltpu.VMEM((ROWS + 2, 2, 8, LON), F32),
            pltpu.VMEM((comps, HALF), F32),
            pltpu.VMEM((comps, HALF), F32),
            pltpu.VMEM((ROWS, comps, LON), BF),
            pltpu.VMEM((ROWS, 1, LON), F32),
            pltpu.VMEM((ROWS, 1, LON), F32),
            pltpu.VMEM((ROWS, 1, LON), F32),
            pltpu.VMEM((ROWS, LON, LON), BF),
            pltpu.VMEM((ROWS, WINDOWS, STRIP, LON), BF),
            pltpu.VMEM((ROWS, NF, LON), BF),
            pltpu.VMEM((GROUPS, SPEC, NF, HALF), BF),
            pltpu.VMEM((GROUPS, SPEC, NF, HALF), BF),
            pltpu.VMEM((GROUPS, SPEC * NF, HALF), F32),
            pltpu.VMEM((SPEC * NF, SPEC * NF), BF),
            pltpu.VMEM((SPEC * NF, SPEC * NF), BF),
            pltpu.VMEM((GROUPS * 2 * SPEC, NF, HALF), BF),
            pltpu.VMEM((ND, 1, ND * NF), F32),
            pltpu.VMEM((GROUPS, SPEC, NF, HALF), BF),
            pltpu.VMEM((GROUPS, SPEC, NF, HALF), BF),
            dma((2, GROUPS)),
            dma((2, GROUPS)),
            dma((2,)),
            dma((2,)),
            dma((GROUPS,)),
            dma((GROUPS,)),
            dma((GROUPS,)),
            dma((GROUPS,)),
            dma((5,)),
            dma((GROUPS,)),
            dma((GROUPS,)),
        ],
        compiler_params=pltpu.CompilerParams(
            collective_id=0, has_side_effects=True, vmem_limit_bytes=64 * 1024 * 1024
        ),
    )(action, east_current, north_current, sea_mask, pattern.T, table)


def solution(mesh):
    return jax.shard_map(
        local,
        mesh=mesh,
        in_specs=(
            P("tile", "spec", None),
            P("tile", None),
            P("tile", None),
            P("tile", None),
            P(),
            P(),
        ),
        out_specs=P("tile", "spec", None),
        check_vma=False,
    )
```

```python
import functools
import math

import jax
import jax.numpy as jnp
from jax import lax
from jax.experimental import pallas as pl
from jax.experimental.pallas import tpu as pltpu
from jax.sharding import PartitionSpec as P

NF = 64
ND = 48
GROUPS = 3
SPEC = 16
TILES = 32
ROWS = 16
LON = 256
HALF = 128
WINDOWS = 8
STRIP = 16
COURANT = 0.45
MESH = pl.DeviceIdType.MESH
BF = jnp.bfloat16
F32 = jnp.float32


def iota(shape, dim):
    return lax.broadcasted_iota(jnp.int32, shape, dim)


def dot(a, b, ca=1, cb=0):
    return lax.dot_general(a, b, (((ca,), (cb,)), ((), ())), preferred_element_type=F32)


def step_kernel(
    action_hbm, east_hbm, north_hbm, mask_hbm, pattern_hbm, table_hbm, out_hbm,
    action, east, north, mask, pattern, table, out, halo, current, coef_e, coef_n, moved, slot_row, window_row, mask_row, onehot, windows, ring,
    send, recv, total, weight_a, weight_b, pairs, hits, back_send, back_recv,
    halo_send, halo_recv, cur_send, cur_recv, out_send, out_recv, ret_send, ret_recv,
    load_sem, action_sem, store_sem,
):
    weight = (weight_a, weight_b)
    me = lax.axis_index("spec")
    tile = lax.axis_index("tile")
    up = lax.rem(tile + 1, TILES)
    down = lax.rem(tile + TILES - 1, TILES)

    barrier = pltpu.get_barrier_semaphore()

    pl.semaphore_signal(barrier, inc=1, device_id={"tile": up}, device_id_type=MESH)
    pl.semaphore_signal(barrier, inc=1, device_id={"tile": down}, device_id_type=MESH)

    def greet(i, carry):
        pl.semaphore_signal(
            barrier, inc=1, device_id={"spec": lax.rem(me + i, SPEC)}, device_id_type=MESH
        )
        return carry

    lax.fori_loop(1, SPEC, greet, 0)

    small = [
        pltpu.make_async_copy(src, dst, load_sem.at[i])
        for i, (src, dst) in enumerate(
            ((east_hbm, east), (north_hbm, north), (mask_hbm, mask), (pattern_hbm, pattern), (table_hbm, table))
        )
    ]
    for copy in small:
        copy.start()

    def group(g):
        return pl.ds(pl.multiple_of(g * NF, NF), NF)

    def action_copy(g):
        return pltpu.make_async_copy(
            action_hbm.at[:, group(g)], action.at[:, group(g)], action_sem.at[g]
        )

    for g in range(GROUPS):
        action_copy(g).start()


    small[0].wait()
    small[1].wait()

    for row in range(ROWS):
        current[row + 1, 0] = jnp.broadcast_to(COURANT * east[row : row + 1, :], (8, LON))
        current[row + 1, 1] = jnp.broadcast_to(COURANT * north[row : row + 1, :], (8, LON))

    pl.semaphore_wait(barrier, SPEC + 1)

    cur_up = pltpu.make_async_remote_copy(
        src_ref=current.at[ROWS], dst_ref=current.at[0],
        send_sem=cur_send.at[0], recv_sem=cur_recv.at[0],
        device_id={"tile": up}, device_id_type=MESH,
    )
    cur_down = pltpu.make_async_remote_copy(
        src_ref=current.at[1], dst_ref=current.at[ROWS + 1],
        send_sem=cur_send.at[1], recv_sem=cur_recv.at[1],
        device_id={"tile": down}, device_id_type=MESH,
    )
    cur_up.start()
    cur_down.start()

    def halo_copies(g):
        comps = group(g)
        to_up = pltpu.make_async_remote_copy(
            src_ref=action_hbm.at[pl.ds(ROWS - 2, 2), comps], dst_ref=halo.at[0, :, comps],
            send_sem=halo_send.at[0, g], recv_sem=halo_recv.at[0, g],
            device_id={"tile": up}, device_id_type=MESH,
        )
        to_down = pltpu.make_async_remote_copy(
            src_ref=action_hbm.at[pl.ds(0, 2), comps], dst_ref=halo.at[1, :, comps],
            send_sem=halo_send.at[1, g], recv_sem=halo_recv.at[1, g],
            device_id={"tile": down}, device_id_type=MESH,
        )
        return to_up, to_down

    def start_halo(g, carry):
        to_up, to_down = halo_copies(g)
        to_up.start()
        to_down.start()
        return carry

    lax.fori_loop(0, GROUPS, start_halo, 0)

    speed = jnp.exp(iota((NF, HALF), 0).astype(F32) * (-2.0 / (NF - 1)))
    for g in range(GROUPS):
        direction = jnp.full((8, HALF), me * GROUPS + g, jnp.int32).astype(F32)
        theta = direction * (2.0 * math.pi / ND)
        cosine = COURANT * jnp.cos(theta)
        sine = COURANT * jnp.sin(theta)
        for k in range(0, NF, 8):
            coef_e[g * NF + k : g * NF + k + 8, :] = speed[k : k + 8] * cosine
            coef_n[g * NF + k : g * NF + k + 8, :] = speed[k : k + 8] * sine

    small[2].wait()
    sea = mask[...].astype(F32)
    sea_b = sea.astype(BF)
    before = (iota((LON, LON), 0) <= iota((LON, LON), 1)).astype(F32).astype(BF)
    rank = dot(sea_b, before)
    count = dot(sea_b, jnp.ones((LON, LON), BF))
    lower = (iota((ROWS, ROWS), 1) < iota((ROWS, ROWS), 0)).astype(F32).astype(BF)
    first = dot(lower, count.astype(BF))
    slot = first + rank - 1.0
    slot_mod = slot - LON * jnp.floor(slot * (1.0 / LON))
    place_at = jnp.where(sea > 0.5, slot_mod, -1.0)
    base = jnp.floor(first * (1.0 / LON))
    lane = iota((ROWS, LON), 1).astype(F32)
    window_at = base + jnp.where(lane < first - LON * base, 1.0, 0.0)
    for row in range(ROWS):
        slot_row[row] = place_at[row : row + 1]
        window_row[row] = window_at[row : row + 1]
        mask_row[row] = sea[row : row + 1]

    def build_row(row, carry):
        place = jnp.broadcast_to(slot_row[row], (LON, LON))
        which = iota((LON, LON), 0).astype(F32)
        onehot[row] = jnp.where(place == which, 1.0, 0.0).astype(BF)
        holds = jnp.broadcast_to(window_row[row], (STRIP, LON))
        for w in range(WINDOWS):
            windows[row, w] = jnp.where(holds == float(w), 1.0, 0.0).astype(BF)
        return carry

    lax.fori_loop(0, ROWS, build_row, 0)

    small[3].wait()
    column = iota((HALF, ND), 0)
    chosen = jnp.zeros((HALF, ND), F32)
    for j in range(ND // 2):
        named = jnp.broadcast_to(pattern[j : j + 1, :], (HALF, ND))
        chosen = chosen + jnp.where(named == column, 1.0, 0.0)
    chosen = chosen.astype(BF)
    for g in range(GROUPS):
        wide = iota((HALF, SPEC * NF), 1)
        spread = (GROUPS * (wide // NF) + g == iota((HALF, SPEC * NF), 0)).astype(F32).astype(BF)
        wide_hits = dot(chosen, spread, 0, 0)
        for r in range(ND):
            hits[r, :, g * SPEC * NF : (g + 1) * SPEC * NF] = wide_hits[r : r + 1]

    small[4].wait()

    def build_pair(s, carry):
        for m in range(GROUPS):
            one = table[GROUPS * s + m]
            two = table[GROUPS * lax.rem(s + 1, SPEC) + m]
            pair = jnp.concatenate([one, two], axis=1)
            pairs[m * 2 * SPEC + s] = pair
            pairs[m * 2 * SPEC + SPEC + s] = pair
        return carry

    lax.fori_loop(0, SPEC, build_pair, 0)

    cur_up.wait()
    cur_down.wait()

    keep_south = jnp.where(tile > 0, 1.0, 0.0).astype(F32)
    keep_north = jnp.where(tile < TILES - 1, 1.0, 0.0).astype(F32)

    def propagate(comp):
        comps = pl.ds(comp, STRIP)
        lane_at = iota((STRIP, HALF), 1)
        first_lane = lane_at == 0
        last_lane = lane_at == HALF - 1
        a_e = coef_e[comps, :]
        a_n = coef_n[comps, :]

        def load(row):
            if row < 0:
                whole = halo[0, row + 2, comps, :] * keep_south.astype(BF)
            elif row >= ROWS:
                whole = halo[1, row - ROWS, comps, :] * keep_north.astype(BF)
            else:
                whole = action[row, comps, :]
            return whole[:, :HALF], whole[:, HALF:]

        def wide(pair):
            return tuple(x.astype(F32) for x in pair)

        def courant(row):
            e = current[row + 1, 0]
            n = current[row + 1, 1]
            res = []
            for h in range(2):
                cols = slice(h * HALF, (h + 1) * HALF)
                ce = a_e + jnp.concatenate([e[:, cols], e[:, cols]], axis=0)
                cn = a_n + jnp.concatenate([n[:, cols], n[:, cols]], axis=0)
                res.append((jnp.abs(ce), ce > 0.0, jnp.abs(cn), cn > 0.0))
            return res

        def turn(pair, shift):
            return tuple(pltpu.roll(x, shift, 1).astype(F32) for x in pair)

        def update(south, here, north_of, speeds, narrow=None):
            wl, wh = turn(narrow or here, 1)
            el, eh = turn(narrow or here, HALF - 1)
            west = (jnp.where(first_lane, 0.0, wl), jnp.where(first_lane, wl, wh))
            east_of = (jnp.where(last_lane, eh, el), jnp.where(last_lane, 0.0, eh))
            res = []
            for h in range(2):
                size_e, pos_e, size_n, pos_n = speeds[h]
                f = here[h]
                from_e = f - jnp.where(pos_e, west[h], east_of[h])
                from_n = f - jnp.where(pos_n, south[h], north_of[h])
                res.append(f - size_e * from_e - size_n * from_n)
            return tuple(res)

        raw = {-2: load(-2), -1: load(-1)}
        f0 = {-2: wide(raw[-2]), -1: wide(raw[-1])}
        f1 = {}
        speeds = {}
        for row in range(-1, ROWS + 1):
            raw[row + 1] = load(row + 1)
            f0[row + 1] = wide(raw[row + 1])
            speeds[row] = courant(row)
            f1[row] = update(f0[row - 1], f0[row], f0[row + 1], speeds[row], raw[row])
            if row == -1:
                f1[row] = tuple(x * keep_south for x in f1[row])
            if row == ROWS:
                f1[row] = tuple(x * keep_north for x in f1[row])
            if row >= 1:
                done = update(f1[row - 2], f1[row - 1], f1[row], speeds[row - 1])
                moved[row - 1, comps, :] = jnp.concatenate(done, axis=1).astype(BF)

    def send_copy(g, peer):
        return pltpu.make_async_remote_copy(
            src_ref=send.at[g, peer], dst_ref=recv.at[g, me],
            send_sem=out_send.at[g], recv_sem=out_recv.at[g],
            device_id={"spec": peer}, device_id_type=MESH,
        )

    def back_copy(g, peer):
        return pltpu.make_async_remote_copy(
            src_ref=back_send.at[g, peer], dst_ref=back_recv.at[g, me],
            send_sem=ret_send.at[g], recv_sem=ret_recv.at[g],
            device_id={"spec": peer}, device_id_type=MESH,
        )

    def all_copies(src, dst, send_sem, recv_sem, g):
        others = pl.ds(0, SPEC - 1)
        return pltpu.make_async_remote_copy(
            src_ref=src.at[g, others], dst_ref=dst.at[g, others],
            send_sem=send_sem.at[g], recv_sem=recv_sem.at[g],
            device_id={"spec": lax.rem(me + 1, SPEC)}, device_id_type=MESH,
        )

    def outgoing(g):
        to_up, to_down = halo_copies(g)
        action_copy(g).wait()
        to_up.wait()
        to_down.wait()
        comps = group(g)

        def strip(s, inner):
            propagate(pl.multiple_of(g * NF + s * STRIP, STRIP))
            return inner

        lax.fori_loop(0, NF // STRIP, strip, 0)

        for row in range(ROWS):
            ring[row] = dot(moved[row, comps, :], onehot[row], 1, 1).astype(BF)

        def gather(w, inner):
            for s in range(NF // STRIP):
                rows = slice(s * STRIP, (s + 1) * STRIP)
                packed = jnp.zeros((STRIP, LON), BF)
                for row in range(ROWS):
                    packed = packed + ring[row, rows, :] * windows[row, w]
                send[g, 2 * w, rows, :] = packed[:, :HALF]
                send[g, 2 * w + 1, rows, :] = packed[:, HALF:]
            return inner

        lax.fori_loop(0, WINDOWS, gather, 0)

        def start(i, inner):
            send_copy(g, lax.rem(me + i, SPEC)).start()
            return inner

        lax.fori_loop(1, SPEC, start, 0)
        recv[g, me] = send[g, me]

    def build_weight(at, q):
        g, h = divmod(at, GROUPS)
        m = (g - h) % GROUPS
        first_pair = m * 2 * SPEC + SPEC - (m + h - g) // GROUPS - q
        for i in range(SPEC // 2):
            col = g * SPEC * NF + i * HALF
            held = hits[GROUPS * q + h, :, col : col + HALF]
            held = jnp.broadcast_to(held, (STRIP, HALF)).astype(BF)
            for k in range(0, NF, STRIP):
                weight[at % 2][q * NF + k : q * NF + k + STRIP, i * HALF : (i + 1) * HALF] = (
                    pairs[first_pair + 2 * i, k : k + STRIP, :] * held
                )

    def couple(g):
        all_copies(send, recv, out_send, out_recv, g).wait_recv()
        cells = recv[g].reshape(SPEC * NF, HALF)
        for h in range(GROUPS):
            at = g * GROUPS + h
            part = dot(weight[at % 2][...], cells)
            if at + 1 < GROUPS * GROUPS:
                for q in range(SPEC):
                    build_weight(at + 1, q)
            if g == 0:
                total[h] = part
            elif g < GROUPS - 1:
                total[h] = total[h] + part
            else:
                coupled = total[h] + part
                own = recv[h].reshape(SPEC * NF, HALF).astype(F32)
                renewed = (own + own * coupled).astype(BF)
                back_send[h] = renewed.reshape(SPEC, NF, HALF)

                def start(i, inner, h=h):
                    back_copy(h, lax.rem(me + i, SPEC)).start()
                    return inner

                lax.fori_loop(1, SPEC, start, 0)
                back_recv[h, me] = back_send[h, me]

    for q in range(SPEC):
        build_weight(0, q)
    for g in range(GROUPS):
        outgoing(g)
    for g in range(GROUPS):
        couple(g)

    def out_copy(h):
        return pltpu.make_async_copy(out.at[:, group(h)], out_hbm.at[:, group(h)], store_sem.at[h])

    def incoming(h, carry):
        all_copies(back_send, back_recv, ret_send, ret_recv, h).wait_recv()
        comps = group(h)

        def pick(row, inner):
            for s in range(NF // STRIP):
                rows = slice(s * STRIP, (s + 1) * STRIP)
                for half in range(2):
                    cols = slice(half * HALF, (half + 1) * HALF)
                    picked = jnp.zeros((STRIP, HALF), BF)
                    for w in range(WINDOWS):
                        picked = picked + back_recv[h, 2 * w + half, rows, :] * windows[row, w, :, cols]
                    ring[row, rows, cols] = picked
            return inner

        lax.fori_loop(0, ROWS, pick, 0)
        for row in range(ROWS):
            wide = dot(ring[row], onehot[row], 1, 0)
            at_sea = jnp.broadcast_to(mask_row[row], (NF, LON)) > 0.5
            result = jnp.where(at_sea, wide, moved[row, comps, :].astype(F32))
            out[row, comps, :] = result.astype(BF)
        out_copy(h).start()
        return carry

    lax.fori_loop(0, GROUPS, incoming, 0)

    def finish(g, carry):
        all_copies(send, recv, out_send, out_recv, g).wait_send()
        all_copies(back_send, back_recv, ret_send, ret_recv, g).wait_send()
        out_copy(g).wait()
        return carry

    lax.fori_loop(0, GROUPS, finish, 0)


def local(action, east_current, north_current, sea_mask, pattern, table):
    hbm = pl.BlockSpec(memory_space=pltpu.HBM)
    dma = pltpu.SemaphoreType.DMA
    comps = GROUPS * NF
    return pl.pallas_call(
        step_kernel,
        out_shape=jax.ShapeDtypeStruct((ROWS, comps, LON), BF),
        in_specs=[hbm] * 6,
        out_specs=hbm,
        scratch_shapes=[
            pltpu.VMEM((ROWS, comps, LON), BF),
            pltpu.VMEM((ROWS, LON), F32),
            pltpu.VMEM((ROWS, LON), F32),
            pltpu.VMEM((ROWS, LON), jnp.int32),
            pltpu.VMEM((ND // 2, ND), jnp.int32),
            pltpu.VMEM((ND, NF, NF), BF),
            pltpu.VMEM((ROWS, comps, LON), BF),
            pltpu.VMEM((2, 2, comps, LON), BF),
            pltpu.VMEM((ROWS + 2, 2, 8, LON), F32),
            pltpu.VMEM((comps, HALF), F32),
            pltpu.VMEM((comps, HALF), F32),
            pltpu.VMEM((ROWS, comps, LON), BF),
            pltpu.VMEM((ROWS, 1, LON), F32),
            pltpu.VMEM((ROWS, 1, LON), F32),
            pltpu.VMEM((ROWS, 1, LON), F32),
            pltpu.VMEM((ROWS, LON, LON), BF),
            pltpu.VMEM((ROWS, WINDOWS, STRIP, LON), BF),
            pltpu.VMEM((ROWS, NF, LON), BF),
            pltpu.VMEM((GROUPS, SPEC, NF, HALF), BF),
            pltpu.VMEM((GROUPS, SPEC, NF, HALF), BF),
            pltpu.VMEM((GROUPS, SPEC * NF, HALF), F32),
            pltpu.VMEM((SPEC * NF, SPEC * NF), BF),
            pltpu.VMEM((SPEC * NF, SPEC * NF), BF),
            pltpu.VMEM((GROUPS * 2 * SPEC, NF, HALF), BF),
            pltpu.VMEM((ND, 1, ND * NF), F32),
            pltpu.VMEM((GROUPS, SPEC, NF, HALF), BF),
            pltpu.VMEM((GROUPS, SPEC, NF, HALF), BF),
            dma((2, GROUPS)),
            dma((2, GROUPS)),
            dma((2,)),
            dma((2,)),
            dma((GROUPS,)),
            dma((GROUPS,)),
            dma((GROUPS,)),
            dma((GROUPS,)),
            dma((5,)),
            dma((GROUPS,)),
            dma((GROUPS,)),
        ],
        compiler_params=pltpu.CompilerParams(
            collective_id=0, has_side_effects=True, vmem_limit_bytes=64 * 1024 * 1024
        ),
    )(action, east_current, north_current, sea_mask, pattern.T, table)


def solution(mesh):
    return jax.shard_map(
        local,
        mesh=mesh,
        in_specs=(
            P("tile", "spec", None),
            P("tile", None),
            P("tile", None),
            P("tile", None),
            P(),
            P(),
        ),
        out_specs=P("tile", "spec", None),
        check_vma=False,
    )
```

```python
import functools
import math

import jax
import jax.numpy as jnp
from jax import lax
from jax.experimental import pallas as pl
from jax.experimental.pallas import tpu as pltpu
from jax.sharding import PartitionSpec as P

NF = 64
ND = 48
GROUPS = 3
SPEC = 16
TILES = 32
ROWS = 16
LON = 256
HALF = 128
WINDOWS = 8
STRIP = 16
COURANT = 0.45
MESH = pl.DeviceIdType.MESH
BF = jnp.bfloat16
F32 = jnp.float32


def iota(shape, dim):
    return lax.broadcasted_iota(jnp.int32, shape, dim)


def dot(a, b, ca=1, cb=0):
    return lax.dot_general(a, b, (((ca,), (cb,)), ((), ())), preferred_element_type=F32)


def step_kernel(
    action_hbm, east_hbm, north_hbm, mask_hbm, pattern_hbm, table_hbm, out_hbm,
    action, east, north, mask, pattern, table, out, halo, current, coef_e, coef_n, moved, slot_row, window_row, mask_row, onehot_t, onehot, windows, ring,
    send, recv, total, weight_a, weight_b, pairs, hits, back_send, back_recv,
    halo_send, halo_recv, cur_send, cur_recv, out_send, out_recv, ret_send, ret_recv,
    load_sem, action_sem, store_sem,
):
    weight = (weight_a, weight_b)
    me = lax.axis_index("spec")
    tile = lax.axis_index("tile")
    up = lax.rem(tile + 1, TILES)
    down = lax.rem(tile + TILES - 1, TILES)

    barrier = pltpu.get_barrier_semaphore()

    pl.semaphore_signal(barrier, inc=1, device_id={"tile": up}, device_id_type=MESH)
    pl.semaphore_signal(barrier, inc=1, device_id={"tile": down}, device_id_type=MESH)

    def greet(i, carry):
        pl.semaphore_signal(
            barrier, inc=1, device_id={"spec": lax.rem(me + i, SPEC)}, device_id_type=MESH
        )
        return carry

    lax.fori_loop(1, SPEC, greet, 0)

    small = [
        pltpu.make_async_copy(src, dst, load_sem.at[i])
        for i, (src, dst) in enumerate(
            ((east_hbm, east), (north_hbm, north), (mask_hbm, mask), (pattern_hbm, pattern), (table_hbm, table))
        )
    ]
    for copy in small:
        copy.start()

    def group(g):
        return pl.ds(pl.multiple_of(g * NF, NF), NF)

    def action_copy(g):
        return pltpu.make_async_copy(
            action_hbm.at[:, group(g)], action.at[:, group(g)], action_sem.at[g]
        )

    for g in range(GROUPS):
        action_copy(g).start()


    small[0].wait()
    small[1].wait()

    for row in range(ROWS):
        current[row + 1, 0] = jnp.broadcast_to(COURANT * east[row : row + 1, :], (8, LON))
        current[row + 1, 1] = jnp.broadcast_to(COURANT * north[row : row + 1, :], (8, LON))

    pl.semaphore_wait(barrier, SPEC + 1)

    cur_up = pltpu.make_async_remote_copy(
        src_ref=current.at[ROWS], dst_ref=current.at[0],
        send_sem=cur_send.at[0], recv_sem=cur_recv.at[0],
        device_id={"tile": up}, device_id_type=MESH,
    )
    cur_down = pltpu.make_async_remote_copy(
        src_ref=current.at[1], dst_ref=current.at[ROWS + 1],
        send_sem=cur_send.at[1], recv_sem=cur_recv.at[1],
        device_id={"tile": down}, device_id_type=MESH,
    )
    cur_up.start()
    cur_down.start()

    def halo_copies(g):
        comps = group(g)
        to_up = pltpu.make_async_remote_copy(
            src_ref=action_hbm.at[pl.ds(ROWS - 2, 2), comps], dst_ref=halo.at[0, :, comps],
            send_sem=halo_send.at[0, g], recv_sem=halo_recv.at[0, g],
            device_id={"tile": up}, device_id_type=MESH,
        )
        to_down = pltpu.make_async_remote_copy(
            src_ref=action_hbm.at[pl.ds(0, 2), comps], dst_ref=halo.at[1, :, comps],
            send_sem=halo_send.at[1, g], recv_sem=halo_recv.at[1, g],
            device_id={"tile": down}, device_id_type=MESH,
        )
        return to_up, to_down

    def start_halo(g, carry):
        to_up, to_down = halo_copies(g)
        to_up.start()
        to_down.start()
        return carry

    lax.fori_loop(0, GROUPS, start_halo, 0)

    speed = jnp.exp(iota((NF, HALF), 0).astype(F32) * (-2.0 / (NF - 1)))
    for g in range(GROUPS):
        direction = jnp.full((8, HALF), me * GROUPS + g, jnp.int32).astype(F32)
        theta = direction * (2.0 * math.pi / ND)
        cosine = COURANT * jnp.cos(theta)
        sine = COURANT * jnp.sin(theta)
        for k in range(0, NF, 8):
            coef_e[g * NF + k : g * NF + k + 8, :] = speed[k : k + 8] * cosine
            coef_n[g * NF + k : g * NF + k + 8, :] = speed[k : k + 8] * sine

    small[2].wait()
    sea = mask[...].astype(F32)
    sea_b = sea.astype(BF)
    before = (iota((LON, LON), 0) <= iota((LON, LON), 1)).astype(F32).astype(BF)
    rank = dot(sea_b, before)
    count = dot(sea_b, jnp.ones((LON, LON), BF))
    lower = (iota((ROWS, ROWS), 1) < iota((ROWS, ROWS), 0)).astype(F32).astype(BF)
    first = dot(lower, count.astype(BF))
    slot = first + rank - 1.0
    slot_mod = slot - LON * jnp.floor(slot * (1.0 / LON))
    place_at = jnp.where(sea > 0.5, slot_mod, -1.0)
    base = jnp.floor(first * (1.0 / LON))
    lane = iota((ROWS, LON), 1).astype(F32)
    window_at = base + jnp.where(lane < first - LON * base, 1.0, 0.0)
    turned = jnp.transpose(place_at)
    across = iota((LON, LON), 1).astype(F32)
    for row in range(ROWS):
        column_at = jnp.broadcast_to(turned[:, row : row + 1], (LON, LON))
        onehot_t[row] = jnp.where(column_at == across, 1.0, 0.0).astype(BF)
        slot_row[row] = place_at[row : row + 1]
        window_row[row] = window_at[row : row + 1]
        mask_row[row] = sea[row : row + 1]

    def build_row(row, carry):
        place = jnp.broadcast_to(slot_row[row], (LON, LON))
        which = iota((LON, LON), 0).astype(F32)
        onehot[row] = jnp.where(place == which, 1.0, 0.0).astype(BF)
        holds = jnp.broadcast_to(window_row[row], (STRIP, LON))
        for w in range(WINDOWS):
            windows[row, w] = jnp.where(holds == float(w), 1.0, 0.0).astype(BF)
        return carry

    lax.fori_loop(0, ROWS, build_row, 0)

    small[3].wait()
    column = iota((HALF, ND), 0)
    chosen = jnp.zeros((HALF, ND), F32)
    for j in range(ND // 2):
        named = jnp.broadcast_to(pattern[j : j + 1, :], (HALF, ND))
        chosen = chosen + jnp.where(named == column, 1.0, 0.0)
    chosen = chosen.astype(BF)
    for g in range(GROUPS):
        wide = iota((HALF, SPEC * NF), 1)
        spread = (GROUPS * (wide // NF) + g == iota((HALF, SPEC * NF), 0)).astype(F32).astype(BF)
        wide_hits = dot(chosen, spread, 0, 0)
        for r in range(ND):
            hits[r, :, g * SPEC * NF : (g + 1) * SPEC * NF] = wide_hits[r : r + 1]

    small[4].wait()

    def build_pair(s, carry):
        for m in range(GROUPS):
            one = table[GROUPS * s + m]
            two = table[GROUPS * lax.rem(s + 1, SPEC) + m]
            pair = jnp.concatenate([one, two], axis=1)
            pairs[m * 2 * SPEC + s] = pair
            pairs[m * 2 * SPEC + SPEC + s] = pair
        return carry

    lax.fori_loop(0, SPEC, build_pair, 0)

    cur_up.wait()
    cur_down.wait()

    keep_south = jnp.where(tile > 0, 1.0, 0.0).astype(F32)
    keep_north = jnp.where(tile < TILES - 1, 1.0, 0.0).astype(F32)

    def propagate(comp):
        comps = pl.ds(comp, STRIP)
        lane_at = iota((STRIP, HALF), 1)
        first_lane = lane_at == 0
        last_lane = lane_at == HALF - 1
        a_e = coef_e[comps, :]
        a_n = coef_n[comps, :]

        def load(row):
            if row < 0:
                whole = halo[0, row + 2, comps, :] * keep_south.astype(BF)
            elif row >= ROWS:
                whole = halo[1, row - ROWS, comps, :] * keep_north.astype(BF)
            else:
                whole = action[row, comps, :]
            return whole[:, :HALF], whole[:, HALF:]

        def wide(pair):
            return tuple(x.astype(F32) for x in pair)

        def courant(row):
            e = current[row + 1, 0]
            n = current[row + 1, 1]
            res = []
            for h in range(2):
                cols = slice(h * HALF, (h + 1) * HALF)
                ce = a_e + jnp.concatenate([e[:, cols], e[:, cols]], axis=0)
                cn = a_n + jnp.concatenate([n[:, cols], n[:, cols]], axis=0)
                res.append((jnp.abs(ce), ce > 0.0, jnp.abs(cn), cn > 0.0))
            return res

        def turn(pair, shift):
            return tuple(pltpu.roll(x, shift, 1).astype(F32) for x in pair)

        def update(south, here, north_of, speeds, narrow=None):
            wl, wh = turn(narrow or here, 1)
            el, eh = turn(narrow or here, HALF - 1)
            west = (jnp.where(first_lane, 0.0, wl), jnp.where(first_lane, wl, wh))
            east_of = (jnp.where(last_lane, eh, el), jnp.where(last_lane, 0.0, eh))
            res = []
            for h in range(2):
                size_e, pos_e, size_n, pos_n = speeds[h]
                f = here[h]
                from_e = f - jnp.where(pos_e, west[h], east_of[h])
                from_n = f - jnp.where(pos_n, south[h], north_of[h])
                res.append(f - size_e * from_e - size_n * from_n)
            return tuple(res)

        raw = {-2: load(-2), -1: load(-1)}
        f0 = {-2: wide(raw[-2]), -1: wide(raw[-1])}
        f1 = {}
        speeds = {}
        for row in range(-1, ROWS + 1):
            raw[row + 1] = load(row + 1)
            f0[row + 1] = wide(raw[row + 1])
            speeds[row] = courant(row)
            f1[row] = update(f0[row - 1], f0[row], f0[row + 1], speeds[row], raw[row])
            if row == -1:
                f1[row] = tuple(x * keep_south for x in f1[row])
            if row == ROWS:
                f1[row] = tuple(x * keep_north for x in f1[row])
            if row >= 1:
                done = update(f1[row - 2], f1[row - 1], f1[row], speeds[row - 1])
                moved[row - 1, comps, :] = jnp.concatenate(done, axis=1).astype(BF)

    def send_copy(g, peer):
        return pltpu.make_async_remote_copy(
            src_ref=send.at[g, peer], dst_ref=recv.at[g, me],
            send_sem=out_send.at[g], recv_sem=out_recv.at[g],
            device_id={"spec": peer}, device_id_type=MESH,
        )

    def back_copy(g, peer):
        return pltpu.make_async_remote_copy(
            src_ref=back_send.at[g, peer], dst_ref=back_recv.at[g, me],
            send_sem=ret_send.at[g], recv_sem=ret_recv.at[g],
            device_id={"spec": peer}, device_id_type=MESH,
        )

    def all_copies(src, dst, send_sem, recv_sem, g):
        others = pl.ds(0, SPEC - 1)
        return pltpu.make_async_remote_copy(
            src_ref=src.at[g, others], dst_ref=dst.at[g, others],
            send_sem=send_sem.at[g], recv_sem=recv_sem.at[g],
            device_id={"spec": lax.rem(me + 1, SPEC)}, device_id_type=MESH,
        )

    def squeeze(g, row):
        lines = moved[row, g * NF : (g + 1) * NF, :]
        ring[row] = dot(lines, onehot_t[row]).astype(BF)

    def advance(g):
        to_up, to_down = halo_copies(g)
        action_copy(g).wait()
        to_up.wait()
        to_down.wait()

        def strip(s, inner):
            if g > 0:
                for k in range(ROWS * STRIP // NF):
                    squeeze(g - 1, s * (ROWS * STRIP // NF) + k)
            propagate(pl.multiple_of(g * NF + s * STRIP, STRIP))
            return inner

        lax.fori_loop(0, NF // STRIP, strip, 0)

    def outgoing(g):
        def gather(w, inner):
            for s in range(NF // STRIP):
                rows = slice(s * STRIP, (s + 1) * STRIP)
                packed = jnp.zeros((STRIP, LON), BF)
                for row in range(ROWS):
                    packed = packed + ring[row, rows, :] * windows[row, w]
                send[g, 2 * w, rows, :] = packed[:, :HALF]
                send[g, 2 * w + 1, rows, :] = packed[:, HALF:]
            return inner

        lax.fori_loop(0, WINDOWS, gather, 0)

        def start(i, inner):
            send_copy(g, lax.rem(me + i, SPEC)).start()
            return inner

        lax.fori_loop(1, SPEC, start, 0)
        recv[g, me] = send[g, me]

    def build_weight(at, q):
        g, h = divmod(at, GROUPS)
        m = (g - h) % GROUPS
        first_pair = m * 2 * SPEC + SPEC - (m + h - g) // GROUPS - q
        for i in range(SPEC // 2):
            col = g * SPEC * NF + i * HALF
            held = hits[GROUPS * q + h, :, col : col + HALF]
            held = jnp.broadcast_to(held, (STRIP, HALF)).astype(BF)
            for k in range(0, NF, STRIP):
                weight[at % 2][q * NF + k : q * NF + k + STRIP, i * HALF : (i + 1) * HALF] = (
                    pairs[first_pair + 2 * i, k : k + STRIP, :] * held
                )

    def couple(g):
        all_copies(send, recv, out_send, out_recv, g).wait_recv()
        cells = recv[g].reshape(SPEC * NF, HALF)
        for h in range(GROUPS):
            at = g * GROUPS + h
            part = dot(weight[at % 2][...], cells)
            if at + 1 < GROUPS * GROUPS:
                for q in range(SPEC):
                    build_weight(at + 1, q)
            if g == 0:
                total[h] = part
            elif g < GROUPS - 1:
                total[h] = total[h] + part
            else:
                coupled = total[h] + part
                own = recv[h].reshape(SPEC * NF, HALF).astype(F32)
                renewed = (own + own * coupled).astype(BF)
                back_send[h] = renewed.reshape(SPEC, NF, HALF)

                def start(i, inner, h=h):
                    back_copy(h, lax.rem(me + i, SPEC)).start()
                    return inner

                lax.fori_loop(1, SPEC, start, 0)
                back_recv[h, me] = back_send[h, me]

    for q in range(SPEC):
        build_weight(0, q)
    for g in range(GROUPS):
        advance(g)
        if g > 0:
            outgoing(g - 1)
    for row in range(ROWS):
        squeeze(GROUPS - 1, row)
    outgoing(GROUPS - 1)
    for g in range(GROUPS):
        couple(g)

    def out_copy(h):
        return pltpu.make_async_copy(out.at[:, group(h)], out_hbm.at[:, group(h)], store_sem.at[h])

    def incoming(h, carry):
        all_copies(back_send, back_recv, ret_send, ret_recv, h).wait_recv()
        comps = group(h)

        def pick(row, inner):
            for s in range(NF // STRIP):
                rows = slice(s * STRIP, (s + 1) * STRIP)
                for half in range(2):
                    cols = slice(half * HALF, (half + 1) * HALF)
                    picked = jnp.zeros((STRIP, HALF), BF)
                    for w in range(WINDOWS):
                        picked = picked + back_recv[h, 2 * w + half, rows, :] * windows[row, w, :, cols]
                    ring[row, rows, cols] = picked
            return inner

        lax.fori_loop(0, ROWS, pick, 0)
        for row in range(ROWS):
            wide = dot(ring[row], onehot[row], 1, 0)
            at_sea = jnp.broadcast_to(mask_row[row], (NF, LON)) > 0.5
            result = jnp.where(at_sea, wide, moved[row, comps, :].astype(F32))
            out[row, comps, :] = result.astype(BF)
        out_copy(h).start()
        return carry

    lax.fori_loop(0, GROUPS, incoming, 0)

    def finish(g, carry):
        all_copies(send, recv, out_send, out_recv, g).wait_send()
        all_copies(back_send, back_recv, ret_send, ret_recv, g).wait_send()
        out_copy(g).wait()
        return carry

    lax.fori_loop(0, GROUPS, finish, 0)


def local(action, east_current, north_current, sea_mask, pattern, table):
    hbm = pl.BlockSpec(memory_space=pltpu.HBM)
    dma = pltpu.SemaphoreType.DMA
    comps = GROUPS * NF
    return pl.pallas_call(
        step_kernel,
        out_shape=jax.ShapeDtypeStruct((ROWS, comps, LON), BF),
        in_specs=[hbm] * 6,
        out_specs=hbm,
        scratch_shapes=[
            pltpu.VMEM((ROWS, comps, LON), BF),
            pltpu.VMEM((ROWS, LON), F32),
            pltpu.VMEM((ROWS, LON), F32),
            pltpu.VMEM((ROWS, LON), jnp.int32),
            pltpu.VMEM((ND // 2, ND), jnp.int32),
            pltpu.VMEM((ND, NF, NF), BF),
            pltpu.VMEM((ROWS, comps, LON), BF),
            pltpu.VMEM((2, 2, comps, LON), BF),
            pltpu.VMEM((ROWS + 2, 2, 8, LON), F32),
            pltpu.VMEM((comps, HALF), F32),
            pltpu.VMEM((comps, HALF), F32),
            pltpu.VMEM((ROWS, comps, LON), BF),
            pltpu.VMEM((ROWS, 1, LON), F32),
            pltpu.VMEM((ROWS, 1, LON), F32),
            pltpu.VMEM((ROWS, 1, LON), F32),
            pltpu.VMEM((ROWS, LON, LON), BF),
            pltpu.VMEM((ROWS, LON, LON), BF),
            pltpu.VMEM((ROWS, WINDOWS, STRIP, LON), BF),
            pltpu.VMEM((ROWS, NF, LON), BF),
            pltpu.VMEM((GROUPS, SPEC, NF, HALF), BF),
            pltpu.VMEM((GROUPS, SPEC, NF, HALF), BF),
            pltpu.VMEM((GROUPS, SPEC * NF, HALF), F32),
            pltpu.VMEM((SPEC * NF, SPEC * NF), BF),
            pltpu.VMEM((SPEC * NF, SPEC * NF), BF),
            pltpu.VMEM((GROUPS * 2 * SPEC, NF, HALF), BF),
            pltpu.VMEM((ND, 1, ND * NF), F32),
            pltpu.VMEM((GROUPS, SPEC, NF, HALF), BF),
            pltpu.VMEM((GROUPS, SPEC, NF, HALF), BF),
            dma((2, GROUPS)),
            dma((2, GROUPS)),
            dma((2,)),
            dma((2,)),
            dma((GROUPS,)),
            dma((GROUPS,)),
            dma((GROUPS,)),
            dma((GROUPS,)),
            dma((5,)),
            dma((GROUPS,)),
            dma((GROUPS,)),
        ],
        compiler_params=pltpu.CompilerParams(
            collective_id=0, has_side_effects=True, vmem_limit_bytes=64 * 1024 * 1024
        ),
    )(action, east_current, north_current, sea_mask, pattern.T, table)


def solution(mesh):
    return jax.shard_map(
        local,
        mesh=mesh,
        in_specs=(
            P("tile", "spec", None),
            P("tile", None),
            P("tile", None),
            P("tile", None),
            P(),
            P(),
        ),
        out_specs=P("tile", "spec", None),
        check_vma=False,
    )
```
